512 devices in a mesh: dp: 32 (over y_lo, z), tensor: 16 (over y_hi, x, core).
Axes of the slice: x: 4, y: 4 (y_hi: 2, y_lo: 2; y = y_hi * 2 + y_lo), z: 16, core: 2. Of those that a mesh axis runs over, the one named last changes fastest.
Arguments:
- inputs: bfloat16 [8192, 6144], P('dp', 'tensor'), may hold values from -250 to 250
- upstream: bfloat16 [8192, 4096], P('dp', 'tensor'), may hold values from -6 to 6
- proj_weight: bfloat16 [6144, 4096], P(None, 'tensor'), may hold values from -0.078125 to 0.078125
- proj_bias: float32 [4096], P('tensor'), may hold values from -4 to 4
- norm_gain: float32 [6144], replicated, may hold values from 0.1 to 1.9
- home_rows: int32 [8192], P('dp'), may hold values from 0 to 8191, as said below
Outputs:
- home_grad: bfloat16 [8192, 6144], P('dp', 'tensor')
The draws below stay inside these ranges and needn't reach their ends.
Inputs may be any that keep to these rules, and one draw needn't show every extreme that they name: `home_rows`: A permutation of 0 to 8191. The balanced row at position i * 256 + k goes to a home row j * 256 + s (0 <= s < 256); of the 256 rows of one dp index, at most 16 have the same owner j, and in every draw some do.
All inputs are finite; a program needn't handle non-finite values.
Results may differ from the reference program's by a relative error of at most 0.018.
Values may be sent and summed in bfloat16 or wider, within the bound.
No kernel may reach another device: no remote copies, remote signals or barrier semaphores. Data moves between devices by JAX's collectives and lax.ppermute only.
A program may use at most 64 MiB of HBM per device.

```python
import math
import jax
import jax.numpy as jnp
from jax import lax

D = 6144
HEAD_DIM = 256
ROW_DEV = 256
CAPACITY = 16
HEADS = 16
COLS = 4096
ROWS = 8192
N_DP = 32


def draw_inputs(key, part):
    first, second, third = jax.random.split(key, 3)
    row_scale = jnp.exp(jax.random.uniform(first, (ROWS, 1), jnp.float32, math.log(0.5), math.log(5.0)))
    col_scale = jnp.exp(jax.random.uniform(second, (1, D), jnp.float32, math.log(0.5), math.log(5.0)))
    return (jax.random.normal(third, (ROWS, D), jnp.float32) * row_scale * col_scale).astype(jnp.bfloat16)


def home_block(key):
    first, second, third = jax.random.split(key, 3)
    identifiers = jnp.arange(N_DP * CAPACITY, dtype=jnp.int32)
    shuffled = jax.random.permutation(first, identifiers)
    placed_at = jnp.zeros((N_DP * CAPACITY,), jnp.int32).at[shuffled].set(identifiers)
    labels = identifiers // CAPACITY
    forced = shuffled[0] // CAPACITY
    ranking = jnp.where(labels == forced, identifiers - N_DP * CAPACITY, placed_at)
    ordering = jnp.argsort(ranking)
    chosen = labels[ordering[:ROW_DEV]]
    offsets = jax.random.permutation(second, chosen)
    within_owner = jax.vmap(lambda subkey: jax.random.permutation(subkey, jnp.arange(ROW_DEV, dtype=jnp.int32)))(jax.random.split(third, N_DP))
    sources = jnp.arange(N_DP, dtype=jnp.int32)[:, None]
    owner_of = (sources + offsets[None, :]) % N_DP
    home_slot = within_owner[owner_of, jnp.arange(ROW_DEV, dtype=jnp.int32)[None, :]]
    return owner_of * ROW_DEV + home_slot


def draw_home_rows(key, part):
    return home_block(key).reshape(-1).astype(jnp.int32)


def with_spikes(drawn, stream_key, source, target, parts, factor):
    owner, partner = [(jnp.arange(drawn.shape[position]) // (drawn.shape[position] // parts)).reshape([-1 if axis == position else 1 for axis in range(drawn.ndim)]) for position in (source, target)]
    chosen = jax.random.permutation(stream_key, parts)[partner]
    strong = (owner == chosen) | (owner == (partner + parts // 2) % parts)
    return jnp.where(strong, factor * drawn, drawn)


def block_levels(own_key, shape, cuts, least, high):
    loudness = 1.0
    for dim, parts in cuts:
        heights = jax.random.uniform(jax.random.fold_in(jax.random.fold_in(own_key, 6), dim), (parts,), jnp.float32, least / len(cuts), high / len(cuts))
        loudness = loudness * jnp.repeat(jnp.exp(heights), shape[dim] // parts).reshape((-1,) + (1,) * (len(shape) - 1 - dim))
    return loudness


def gaussian(own_key, shape, width, bound, shards=(), kind=jnp.bfloat16):
    values = width * jax.random.normal(own_key, shape, jnp.float32)
    if shards:
        values = values * block_levels(own_key, shape, shards, -0.22, 0.18)
    return jnp.clip(values, -bound, bound).astype(kind)


def heavy_noise(rng, extent, width, limit, cuts, heavy, kind=jnp.bfloat16):
    values = width * jax.random.normal(rng, extent, jnp.float32)
    if cuts:
        values = values * block_levels(rng, extent, cuts, -0.22, 0.18)
    return jnp.clip(with_spikes(values, jax.random.fold_in(rng, 3), *heavy), -limit, limit).astype(kind)


def setup_inputs(seed: int = 0) -> dict:
    key_of = jax.random.split(jax.random.key(seed), 7)
    inputs = draw_inputs(jax.random.fold_in(key_of[6], 71), 0)
    upstream = heavy_noise(key_of[1], (ROWS, COLS), 1.0, 6.0, ((0, 32), (1, 16)), (1, 0, 32, 2.75))
    proj_weight = gaussian(key_of[2], (D, COLS), D ** -0.5, 0.078125, ((1, 16),))
    proj_bias = gaussian(key_of[3], (COLS,), 1.0, 4.0, ((0, 16),), jnp.float32)
    norm_gain = jnp.clip(1.0 + 0.18 * jax.random.normal(key_of[4], (D,), jnp.float32), 0.1, 1.9)
    home_rows = draw_home_rows(jax.random.fold_in(key_of[6], 71), 0)
    return dict(inputs=inputs, upstream=upstream, proj_weight=proj_weight, proj_bias=proj_bias, norm_gain=norm_gain, home_rows=home_rows)


epsilon = 1e-05

def contract_cols(left, right):
    return lax.dot_general(left.astype(jnp.float32), right.astype(jnp.float32), (((1,), (1,)), ((), ())), preferred_element_type=jnp.float32)

def reference(inputs, upstream, proj_weight, proj_bias, norm_gain, home_rows):
    widened = inputs.astype(jnp.float32)
    row_mean = lax.optimization_barrier(jnp.mean(widened, axis=1, keepdims=True))
    centred = widened - row_mean
    inv_std = lax.rsqrt(lax.optimization_barrier(jnp.mean(centred * centred, axis=1, keepdims=True)) + epsilon)
    unit_rows = centred * inv_std
    normed = (unit_rows * norm_gain[None, :]).astype(jnp.bfloat16)
    preact = jnp.dot(normed, proj_weight, preferred_element_type=jnp.float32) + proj_bias[None, :]
    gate_value = jax.nn.sigmoid(preact)
    pre_grad = (upstream.astype(jnp.float32) * gate_value * (1.0 + preact * (1.0 - gate_value))).astype(jnp.bfloat16)

    def add_head(head, total):
        start = (head * HEAD_DIM).astype(jnp.int32)
        part_grad = lax.dynamic_slice_in_dim(pre_grad, start, HEAD_DIM, 1)
        part_weight = lax.dynamic_slice_in_dim(proj_weight, start, HEAD_DIM, 1)
        term = contract_cols(part_grad, part_weight).astype(jnp.bfloat16)
        return total + lax.optimization_barrier(term).astype(jnp.float32)
    summed = lax.fori_loop(0, HEADS, add_head, jnp.zeros((ROWS, D), jnp.float32))
    scaled = summed * norm_gain[None, :]
    input_grad = (inv_std * (scaled - lax.optimization_barrier(jnp.mean(scaled, axis=1, keepdims=True)) - unit_rows * lax.optimization_barrier(jnp.mean(scaled * unit_rows, axis=1, keepdims=True)))).astype(jnp.bfloat16)
    return jnp.zeros((ROWS, D), jnp.bfloat16).at[home_rows.astype(jnp.int32)].set(input_grad)
```

```python
import jax
import jax.numpy as jnp
from jax import lax
from jax.experimental import pallas as pl
from jax.experimental.pallas import tpu as pltpu
from jax.sharding import PartitionSpec as P

epsilon = 1e-05
f32, bf16 = jnp.float32, jnp.bfloat16
PAD = 16
NT = (((1,), (1,)), ((), ()))


def in_vmem(n):
    return [pl.BlockSpec(memory_space=pltpu.VMEM) for _ in range(n)]


SCALAR = pl.BlockSpec(memory_space=pltpu.SMEM)


def forward_kernel(core_ref, x_ref, gain_ref, weight_ref, other_ref, q_ref):
    blocks, rows, feats = x_ref.shape
    width = other_ref.shape[2]
    core = core_ref[0]
    total = jnp.zeros((rows, 1), f32)
    for b in range(blocks):
        total += jnp.sum(x_ref[b].astype(f32), axis=1, keepdims=True)
    mean = total / (blocks * feats)
    spread = jnp.zeros((rows, 1), f32)
    own = jnp.zeros((rows, width), f32)
    other = jnp.zeros((rows, width), f32)
    for b in range(blocks):
        centred = x_ref[b].astype(f32) - mean
        spread += jnp.sum(centred * centred, axis=1, keepdims=True)
        scaled = (centred * gain_ref[b, core]).astype(bf16)
        own += jnp.dot(scaled, weight_ref[b, core], preferred_element_type=f32)
        other += jnp.dot(scaled, other_ref[b], preferred_element_type=f32)
    q_ref[:, :width] = own
    q_ref[:, width : 2 * width] = other
    lane = lax.broadcasted_iota(jnp.int32, (rows, 128), 1)
    q_ref[:, 2 * width :] = jnp.where(lane == 0, mean, spread / (blocks * feats))


def forward(core, x, gain, weight, other):
    blocks, rows, feats = x.shape
    width = other.shape[2]
    return pl.pallas_call(
        forward_kernel,
        in_specs=[SCALAR] + in_vmem(4),
        out_specs=in_vmem(1)[0],
        out_shape=jax.ShapeDtypeStruct((rows, 2 * width + 128), f32),
        name="forward",
    )(core, x, gain, weight, other)


def backward_kernel(
    core_ref, q_ref, got_ref, up_ref, upo_ref, vec_ref, veco_ref, weight_ref, other_ref, p_ref, st_ref
):
    blocks, feats, width = other_ref.shape
    rows = q_ref.shape[0]
    core = core_ref[0]
    mine, theirs = q_ref[:, 2 * width :], got_ref[:, 2 * width :]
    mean_here, mean_there = mine[:, 0:1], theirs[:, 0:1]
    gap = 0.5 * (mean_here - mean_there)
    mean = 0.5 * (mean_here + mean_there)
    variance = 0.5 * (mine[:, 1:2] + theirs[:, 1:2]) + gap * gap
    inv_std = lax.rsqrt(variance + epsilon)
    lane = lax.broadcasted_iota(jnp.int32, (rows, 128), 1)
    st_ref[...] = jnp.where(lane == 0, mean, inv_std)
    side = jnp.where(core == 0, 1.0, -1.0)

    def grad(summed, up, vec):
        raw = inv_std * (summed + gap * (side * (vec[1:2, :] - vec[2:3, :])))
        preact = raw + vec[0:1, :]
        gate = 1.0 / (1.0 + jnp.exp(-preact))
        pg = (up.astype(f32) * gate * (1.0 + preact * (1.0 - gate))).astype(bf16)
        wide = pg.astype(f32)
        scale = jnp.broadcast_to(vec[1:2, :] + vec[2:3, :], (8, width))
        first = lax.dot_general(scale, wide, NT, precision=lax.Precision.HIGHEST)
        second = lax.dot_general(
            jnp.ones((8, width), f32), wide * raw, NT, precision=lax.Precision.HIGHEST
        )
        return pg, first, second

    pg, first, second = grad(q_ref[:, :width] + got_ref[:, width : 2 * width], up_ref[...], vec_ref[...])
    pgo, firsto, secondo = grad(
        q_ref[:, width : 2 * width] + got_ref[:, :width], upo_ref[...], veco_ref[...]
    )
    first, second = first + firsto, second + secondo
    row = lax.broadcasted_iota(jnp.int32, (8, rows), 0)
    value = jnp.where(row < 2, first, second)
    high = value.astype(bf16).astype(f32)
    tail = jnp.where(row % 2 == 0, high, value - high)
    tail = jnp.concatenate([tail, jnp.zeros_like(tail)], axis=0).astype(bf16)
    tail = jnp.concatenate([tail, jnp.zeros((PAD, feats - rows), bf16)], axis=1)
    for b in range(blocks):
        p_ref[b, :rows] = (
            lax.dot_general(pg, weight_ref[b, core], NT, preferred_element_type=f32)
            + lax.dot_general(pgo, other_ref[b], NT, preferred_element_type=f32)
        ).astype(bf16)
        p_ref[b, rows:] = tail


def backward(core, q, got, up, upo, vec, veco, weight, other):
    blocks, feats, width = other.shape
    rows = q.shape[0]
    return pl.pallas_call(
        backward_kernel,
        in_specs=[SCALAR] + in_vmem(8),
        out_specs=in_vmem(2),
        out_shape=[
            jax.ShapeDtypeStruct((blocks, rows + PAD, feats), bf16),
            jax.ShapeDtypeStruct((rows, 128), f32),
        ],
        name="backward",
    )(core, q, got, up, upo, vec, veco, weight, other)


def finish_kernel(back_ref, x_ref, st_ref, gain_ref, target_ref, send_ref):
    blocks = back_ref.shape[0]
    rows, feats = x_ref.shape
    slots = send_ref.shape[0]
    total = back_ref[0].astype(f32)
    for b in range(1, blocks):
        total += back_ref[b].astype(f32)
    tail = total[rows : rows + 8, :rows]
    sums = tail.T / (2 * blocks * feats)
    first = sums[:, 0:1] + sums[:, 1:2]
    second = sums[:, 2:3] + sums[:, 3:4]
    mean, inv_std = st_ref[:, 0:1], st_ref[:, 1:2]
    unit = (x_ref[...].astype(f32) - mean) * inv_std
    grad = (inv_std * (total[:rows] * gain_ref[...] - first - unit * second)).astype(bf16)
    placing = lax.broadcasted_iota(jnp.int32, (slots, rows), 0) == target_ref[...]
    send_ref[...] = jnp.dot(
        jnp.where(placing, 1.0, 0.0).astype(bf16), grad, preferred_element_type=f32
    ).astype(bf16)


def finish(back, x, st, gain, target, slots):
    return pl.pallas_call(
        finish_kernel,
        in_specs=in_vmem(5),
        out_specs=in_vmem(1)[0],
        out_shape=jax.ShapeDtypeStruct((slots, x.shape[1]), bf16),
        name="finish",
    )(back, x, st, gain, target)


def landing_kernel(got_ref, slot_ref, o_ref):
    rows = o_ref.shape[0]
    slots = got_ref.shape[0]
    landing = lax.broadcasted_iota(jnp.int32, (rows, slots), 0) == slot_ref[...]
    o_ref[...] = jnp.dot(
        jnp.where(landing, 1.0, 0.0).astype(bf16), got_ref[...], preferred_element_type=f32
    ).astype(bf16)


def land(got, slot, rows):
    return pl.pallas_call(
        landing_kernel,
        in_specs=in_vmem(2),
        out_specs=in_vmem(1)[0],
        out_shape=jax.ShapeDtypeStruct((rows, got.shape[1]), bf16),
        name="land",
    )(got, slot)


def per_device(inputs, upstream, proj_weight, proj_bias, norm_gain, home_rows):
    rows, feats = inputs.shape
    width = upstream.shape[1]
    n_tensor, owners = lax.axis_size("tensor"), lax.axis_size("dp")
    chips = n_tensor // 2
    me = lax.axis_index("tensor")
    core = me % 2
    swap = [(t, t ^ 1) for t in range(n_tensor)]
    classes = [[2 * k + c for k in range(chips)] for c in range(2)]
    core_arr = core.reshape(1).astype(jnp.int32)

    sent = jnp.broadcast_to(inputs[None], (chips, rows, feats))
    half = lax.all_to_all(sent, "tensor", 0, 0, axis_index_groups=classes, tiled=True)

    pairs = proj_weight.reshape(chips, 2, feats, width)
    other = lax.ppermute(lax.dynamic_index_in_dim(pairs, 1 - core, 1, False), "tensor", swap)
    upo = lax.ppermute(upstream, "tensor", swap)
    gains = norm_gain.reshape(chips, 2, 1, feats)
    scales = jnp.sum(norm_gain.reshape(chips, 2, feats, 1) * pairs.astype(f32), axis=(0, 2))
    vec = jnp.concatenate([proj_bias[None], scales], axis=0)
    veco = lax.ppermute(vec, "tensor", swap)

    capacity = max(2, 2 * rows // owners)
    owner_of = home_rows // rows
    home_slot = home_rows % rows
    order_ids = jnp.arange(rows, dtype=jnp.int32)
    earlier = jnp.sum(
        ((owner_of[:, None] == owner_of[None, :]) & (order_ids[:, None] > order_ids[None, :])).astype(
            jnp.int32
        ),
        axis=1,
    )
    target = owner_of * capacity + earlier
    placing = jnp.arange(owners * capacity, dtype=jnp.int32)[:, None] == target[None, :]
    send_slots = jnp.sum(jnp.where(placing, home_slot[None, :] + 1, 0), axis=1) - 1
    arrived_slots = lax.all_to_all(
        send_slots.reshape(owners, 1, capacity), "dp", split_axis=0, concat_axis=0, tiled=True
    ).reshape(1, -1)

    half, other, upo, veco, arrived_slots, target = lax.optimization_barrier(
        (half, other, upo, veco, arrived_slots, target)
    )
    q = forward(core_arr, half, gains, pairs, other)
    got = lax.ppermute(q, "tensor", swap)
    parts, st = backward(core_arr, q, got, upstream, upo, vec, veco, pairs, other)
    back = lax.all_to_all(parts, "tensor", 0, 0, axis_index_groups=classes, tiled=True)
    own_gain = lax.dynamic_index_in_dim(norm_gain.reshape(n_tensor, 1, feats), me, 0, False)
    send_rows = finish(back, inputs, st, own_gain, target[None, :], owners * capacity)
    arrived = lax.all_to_all(send_rows, "dp", split_axis=0, concat_axis=0, tiled=True)
    return land(arrived, arrived_slots, rows)


def solution(mesh):
    return jax.shard_map(
        per_device,
        mesh=mesh,
        in_specs=(
            P("dp", "tensor"),
            P("dp", "tensor"),
            P(None, "tensor"),
            P("tensor"),
            P(),
            P("dp"),
        ),
        out_specs=P("dp", "tensor"),
        check_vma=False,
    )
```

```python
import jax
import jax.numpy as jnp
from jax import lax
from jax.experimental import pallas as pl
from jax.experimental.pallas import tpu as pltpu
from jax.sharding import PartitionSpec as P


epsilon = 1e-05
f32, bf16 = jnp.float32, jnp.bfloat16
PAD = 16
CAPACITY = 16
NT = (((1,), (1,)), ((), ()))


def in_vmem(n):
    return [pl.BlockSpec(memory_space=pltpu.VMEM) for _ in range(n)]


def held(*arrays):
    return [pltpu.with_memory_space_constraint(a, pltpu.VMEM) for a in arrays]


PARAMS = pltpu.CompilerParams(vmem_limit_bytes=16 * 1024 * 1024)


ANYWHERE = pl.BlockSpec(memory_space=pl.ANY)
SCALAR = pl.BlockSpec(memory_space=pltpu.SMEM)


def forward_kernel(
    core_ref, x_any, gain_ref, weight_any, other_any, q_ref, x_ref, weight_ref, other_ref, x_sem, w_sem, o_sem
):
    blocks, rows, feats = x_ref.shape
    width = other_ref.shape[2]
    core = core_ref[0]
    x_copies = [pltpu.make_async_copy(x_any.at[b], x_ref.at[b], x_sem.at[b]) for b in range(blocks)]
    w_copies = [
        pltpu.make_async_copy(weight_any.at[b, core], weight_ref.at[b], w_sem.at[b]) for b in range(blocks)
    ]
    o_copies = [
        pltpu.make_async_copy(other_any.at[b], other_ref.at[b], o_sem.at[b]) for b in range(blocks)
    ]
    for copy in x_copies:
        copy.start()
    for b in range(blocks):
        w_copies[b].start()
        o_copies[b].start()
    total = jnp.zeros((rows, feats), f32)
    for b in range(blocks):
        x_copies[b].wait()
        total += x_ref[b].astype(f32)
    mean = jnp.sum(total, axis=1, keepdims=True) / (blocks * feats)
    spread = jnp.zeros((rows, feats), f32)
    for b in range(blocks):
        centred = x_ref[b].astype(f32) - mean
        spread += centred * centred
        scaled = (centred * gain_ref[b, core]).astype(bf16)
        w_copies[b].wait()
        o_copies[b].wait()
        own = jnp.dot(scaled, weight_ref[b], preferred_element_type=f32)
        other = jnp.dot(scaled, other_ref[b], preferred_element_type=f32)
        if b == 0:
            q_ref[:, :width] = own
            q_ref[:, width : 2 * width] = other
        else:
            q_ref[:, :width] += own
            q_ref[:, width : 2 * width] += other
    spread = jnp.sum(spread, axis=1, keepdims=True) / (blocks * feats)
    lane = lax.broadcasted_iota(jnp.int32, (rows, 128), 1)
    q_ref[:, 2 * width :] = jnp.where(lane == 0, mean, spread)


def forward(core, x, gain, weight, other):
    blocks, rows, _ = x.shape
    width = other.shape[2]
    return pl.pallas_call(
        forward_kernel,
        in_specs=[SCALAR, ANYWHERE] + in_vmem(1) + [ANYWHERE, ANYWHERE],
        out_specs=in_vmem(1)[0],
        out_shape=jax.ShapeDtypeStruct((rows, 2 * width + 128), f32),
        scratch_shapes=[
            pltpu.VMEM(x.shape, bf16),
            pltpu.VMEM(other.shape, bf16),
            pltpu.VMEM(other.shape, bf16),
            pltpu.SemaphoreType.DMA((blocks,)),
            pltpu.SemaphoreType.DMA((blocks,)),
            pltpu.SemaphoreType.DMA((blocks,)),
        ],
        compiler_params=PARAMS,
        name="forward",
    )(core, x, gain, weight, other)


def backward_kernel(
    core_ref,
    q_ref,
    got_ref,
    up_ref,
    upo_ref,
    vec_ref,
    veco_ref,
    weight_any,
    other_any,
    p_any,
    st_ref,
    weight_ref,
    other_ref,
    p_ref,
    w_sem,
    o_sem,
    p_sem,
):
    blocks, feats, width = other_ref.shape
    rows = q_ref.shape[0]
    core = core_ref[0]
    w_copies = [
        pltpu.make_async_copy(weight_any.at[b, core], weight_ref.at[b], w_sem.at[b]) for b in range(blocks)
    ]
    o_copies = [
        pltpu.make_async_copy(other_any.at[b], other_ref.at[b], o_sem.at[b]) for b in range(blocks)
    ]
    p_copies = [pltpu.make_async_copy(p_ref.at[b], p_any.at[b], p_sem.at[b]) for b in range(blocks)]
    for b in range(blocks):
        w_copies[b].start()
        o_copies[b].start()
    mine, theirs = q_ref[:, 2 * width :], got_ref[:, 2 * width :]
    mean_here, mean_there = mine[:, 0:1], theirs[:, 0:1]
    gap = 0.5 * (mean_here - mean_there)
    mean = 0.5 * (mean_here + mean_there)
    variance = 0.5 * (mine[:, 1:2] + theirs[:, 1:2]) + gap * gap
    inv_std = lax.rsqrt(variance + epsilon)
    lane = lax.broadcasted_iota(jnp.int32, (rows, 128), 1)
    st_ref[...] = jnp.where(lane == 0, mean, inv_std)
    side = jnp.where(core == 0, 1.0, -1.0)

    def grad(summed, up, vec):
        raw = inv_std * (summed + gap * (side * (vec[1:2, :] - vec[2:3, :])))
        preact = raw + vec[0:1, :]
        gate = 1.0 / (1.0 + jnp.exp(-preact))
        pg = (up.astype(f32) * gate * (1.0 + preact * (1.0 - gate))).astype(bf16)
        wide = pg.astype(f32)
        scale = jnp.broadcast_to(vec[1:2, :] + vec[2:3, :], (8, width))
        first = lax.dot_general(scale, wide, NT, precision=lax.Precision.HIGHEST)
        second = lax.dot_general(
            jnp.ones((8, width), f32), wide * raw, NT, precision=lax.Precision.HIGHEST
        )
        return pg, first, second

    pg, first, second = grad(q_ref[:, :width] + got_ref[:, width : 2 * width], up_ref[...], vec_ref[...])
    pgo, firsto, secondo = grad(
        q_ref[:, width : 2 * width] + got_ref[:, :width], upo_ref[...], veco_ref[...]
    )
    first, second = first + firsto, second + secondo
    row = lax.broadcasted_iota(jnp.int32, (8, rows), 0)
    value = jnp.where(row < 2, first, second)
    high = value.astype(bf16).astype(f32)
    tail = jnp.where(row % 2 == 0, high, value - high)
    tail = jnp.concatenate([tail, jnp.zeros_like(tail)], axis=0).astype(bf16)
    tail = jnp.concatenate([tail, jnp.zeros((PAD, feats - rows), bf16)], axis=1)
    for b in range(blocks):
        w_copies[b].wait()
        o_copies[b].wait()
        p_ref[b, :rows] = (
            lax.dot_general(pg, weight_ref[b], NT, preferred_element_type=f32)
            + lax.dot_general(pgo, other_ref[b], NT, preferred_element_type=f32)
        ).astype(bf16)
        p_ref[b, rows:] = tail
        p_copies[b].start()
    for copy in p_copies:
        copy.wait()


def backward(core, q, got, up, upo, vec, veco, weight, other):
    blocks, feats, _ = other.shape
    rows = q.shape[0]
    return pl.pallas_call(
        backward_kernel,
        in_specs=[SCALAR] + in_vmem(6) + [ANYWHERE, ANYWHERE],
        out_specs=[ANYWHERE] + in_vmem(1),
        out_shape=[
            jax.ShapeDtypeStruct((blocks, rows + PAD, feats), bf16),
            jax.ShapeDtypeStruct((rows, 128), f32),
        ],
        scratch_shapes=[
            pltpu.VMEM(other.shape, bf16),
            pltpu.VMEM(other.shape, bf16),
            pltpu.VMEM((blocks, rows + PAD, feats), bf16),
            pltpu.SemaphoreType.DMA((blocks,)),
            pltpu.SemaphoreType.DMA((blocks,)),
            pltpu.SemaphoreType.DMA((blocks,)),
        ],
        compiler_params=PARAMS,
        name="backward",
    )(core, q, got, up, upo, vec, veco, weight, other)


def finish_kernel(back_ref, x_ref, st_ref, gain_ref, target_ref, slot_ref, send_ref):
    blocks = back_ref.shape[0]
    rows, feats = x_ref.shape
    owners = send_ref.shape[0]
    total = back_ref[0].astype(f32)
    for b in range(1, blocks):
        total += back_ref[b].astype(f32)
    tail = total[rows : rows + 8, :rows]
    sums = tail.T / (2 * blocks * feats)
    first = sums[:, 0:1] + sums[:, 1:2]
    second = sums[:, 2:3] + sums[:, 3:4]
    mean, inv_std = st_ref[:, 0:1], st_ref[:, 1:2]
    unit = (x_ref[...].astype(f32) - mean) * inv_std
    grad = (inv_std * (total[:rows] * gain_ref[...] - first - unit * second)).astype(bf16)
    slots = owners * CAPACITY
    placing = lax.broadcasted_iota(jnp.int32, (slots, rows), 0) == target_ref[...]
    placed = jnp.dot(
        jnp.where(placing, 1.0, 0.0).astype(bf16), grad, preferred_element_type=f32
    ).astype(bf16)
    placed = placed.reshape(owners, CAPACITY, feats)
    for k in range(feats // 128):
        send_ref[:, k * CAPACITY : (k + 1) * CAPACITY, :] = placed[:, :, k * 128 : (k + 1) * 128]
    send_ref[:, feats // 128 * CAPACITY :, :] = jnp.broadcast_to(slot_ref[...][:, None, :], (owners, 8, 128))


def finish(back, x, st, gain, target, slot):
    owners = slot.shape[0]
    return pl.pallas_call(
        finish_kernel,
        in_specs=in_vmem(6),
        out_specs=in_vmem(1)[0],
        out_shape=pltpu.VMEM((owners, x.shape[1] // 128 * CAPACITY + 8, 128), bf16),
        compiler_params=PARAMS,
        name="finish",
    )(*held(back, x, st, gain, target, slot))


def landing_kernel(got_ref, o_ref):
    rows, feats = o_ref.shape
    owners = got_ref.shape[0]
    slots = owners * CAPACITY
    pieces = feats // 128
    held_slots = got_ref[:, pieces * CAPACITY, :].astype(bf16)
    spread = lax.broadcasted_iota(jnp.int32, (128, slots), 0) == (
        lax.broadcasted_iota(jnp.int32, (128, slots), 1) % CAPACITY
    )
    every = jnp.dot(held_slots, jnp.where(spread, 1.0, 0.0).astype(bf16), preferred_element_type=f32)
    own = lax.broadcasted_iota(jnp.int32, (owners, slots), 0) == (
        lax.broadcasted_iota(jnp.int32, (owners, slots), 1) // CAPACITY
    )
    slot = jnp.sum(jnp.where(own, every, 0.0), axis=0, keepdims=True).astype(jnp.int32)
    landing = lax.broadcasted_iota(jnp.int32, (rows, slots), 0) == slot
    landing = jnp.where(landing, 1.0, 0.0).astype(bf16)
    for k in range(pieces):
        piece = got_ref[:, k * CAPACITY : (k + 1) * CAPACITY, :].reshape(slots, 128)
        o_ref[:, k * 128 : (k + 1) * 128] = jnp.dot(
            landing, piece, preferred_element_type=f32
        ).astype(bf16)


def land(got, rows, feats):
    return pl.pallas_call(
        landing_kernel,
        in_specs=in_vmem(1),
        out_specs=in_vmem(1)[0],
        out_shape=jax.ShapeDtypeStruct((rows, feats), bf16),
        compiler_params=PARAMS,
        name="land",
    )(*held(got))


def per_device(inputs, upstream, proj_weight, proj_bias, norm_gain, home_rows):
    rows, feats = inputs.shape
    width = upstream.shape[1]
    n_tensor, owners = lax.axis_size("tensor"), lax.axis_size("dp")
    chips = n_tensor // 2
    me = lax.axis_index("tensor")
    core = me % 2
    swap = [(t, t ^ 1) for t in range(n_tensor)]
    classes = [[2 * k + c for k in range(chips)] for c in range(2)]
    core_arr = core.reshape(1).astype(jnp.int32)

    sent = jnp.broadcast_to(inputs[None], (chips, rows, feats))
    half = lax.all_to_all(sent, "tensor", 0, 0, axis_index_groups=classes, tiled=True)

    pairs = proj_weight.reshape(chips, 2, feats, width)
    cut = lax.dynamic_index_in_dim(pairs, 1 - core, 1, False)
    other = lax.ppermute(cut, "tensor", swap)
    upo = lax.ppermute(upstream, "tensor", swap)
    gains = norm_gain.reshape(chips, 2, 1, feats)
    scales = jnp.sum(norm_gain.reshape(chips, 2, feats, 1) * pairs.astype(f32), axis=(0, 2))
    vec = jnp.concatenate([proj_bias[None], scales], axis=0)
    veco = lax.ppermute(vec, "tensor", swap)

    owner_of = home_rows // rows
    home_slot = home_rows % rows
    order_ids = jnp.arange(rows, dtype=jnp.int32)
    earlier = jnp.sum(
        ((owner_of[:, None] == owner_of[None, :]) & (order_ids[:, None] > order_ids[None, :])).astype(
            jnp.int32
        ),
        axis=1,
    )
    target = owner_of * CAPACITY + earlier
    lanes = jnp.arange(128, dtype=jnp.int32)
    held_at = (jnp.arange(owners, dtype=jnp.int32)[:, None] * CAPACITY + lanes[None, :])[:, :, None]
    match = (held_at == target[None, None, :]) & (lanes < CAPACITY)[None, :, None]
    slot = jnp.sum(jnp.where(match, home_slot[None, None, :] + 1, 0), axis=2) - 1
    slot = slot.astype(f32).astype(bf16)

    own_gain = lax.dynamic_index_in_dim(norm_gain.reshape(n_tensor, 1, feats), me, 0, False)
    half, other, upo, veco, slot, target, own_gain = lax.optimization_barrier(
        (half, other, upo, veco, slot, target, own_gain)
    )
    q = forward(core_arr, half, gains, pairs, other)
    got = lax.ppermute(q, "tensor", swap)
    parts, st = backward(core_arr, q, got, upstream, upo, vec, veco, pairs, other)
    back = lax.all_to_all(parts, "tensor", 0, 0, axis_index_groups=classes, tiled=True)
    send = finish(back, inputs, st, own_gain, target[None, :], slot)
    arrived = lax.all_to_all(send, "dp", split_axis=0, concat_axis=0, tiled=True)
    return land(arrived, rows, feats)


def solution(mesh):
    return jax.shard_map(
        per_device,
        mesh=mesh,
        in_specs=(
            P("dp", "tensor"),
            P("dp", "tensor"),
            P(None, "tensor"),
            P("tensor"),
            P(),
            P("dp"),
        ),
        out_specs=P("dp", "tensor"),
        check_vma=False,
    )
```

```python
import jax
import jax.numpy as jnp
from jax import lax
from jax.experimental import pallas as pl
from jax.experimental.pallas import tpu as pltpu
from jax.sharding import PartitionSpec as P


epsilon = 1e-05
f32, bf16 = jnp.float32, jnp.bfloat16
PAD = 16
CAPACITY = 16
NT = (((1,), (1,)), ((), ()))


def in_vmem(n):
    return [pl.BlockSpec(memory_space=pltpu.VMEM) for _ in range(n)]


def held(*arrays):
    return [pltpu.with_memory_space_constraint(a, pltpu.VMEM) for a in arrays]


PARAMS = pltpu.CompilerParams(vmem_limit_bytes=16 * 1024 * 1024)


ANYWHERE = pl.BlockSpec(memory_space=pl.ANY)
SCALAR = pl.BlockSpec(memory_space=pltpu.SMEM)


def weight_copies(core, first, weight_any, other_any, weight_ref, w_sem, o_sem):
    slots, _, width = weight_ref.shape
    blocks = other_any.shape[0]
    copies = []
    for p in range(slots):
        k = (first + p) % blocks
        copies.append(
            (
                pltpu.make_async_copy(
                    weight_any.at[k, core], weight_ref.at[p, :, : width // 2], w_sem.at[p]
                ),
                pltpu.make_async_copy(other_any.at[k], weight_ref.at[p, :, width // 2 :], o_sem.at[p]),
            )
        )
    return copies


def forward_kernel(
    place_ref, near_any, far_any, gain_ref, weight_any, other_any, q_ref, x_ref, weight_ref, x_sem, w_sem, o_sem
):
    blocks, rows, feats = x_ref.shape
    width = weight_ref.shape[2]
    half = blocks // 2
    core, first = place_ref[0], place_ref[1]
    x_copies = [
        pltpu.make_async_copy((near_any if p < half else far_any).at[p % half], x_ref.at[p], x_sem.at[p])
        for p in range(blocks)
    ]
    w_copies = weight_copies(core, first, weight_any, other_any, weight_ref, w_sem, o_sem)
    for copy in x_copies:
        copy.start()
    for pair in w_copies:
        for copy in pair:
            copy.start()
    total = jnp.zeros((rows, 128), f32)
    for p in range(blocks):
        x_copies[p].wait()
        for j in range(0, feats, 128):
            total += x_ref[p, :, j : j + 128].astype(f32)
    mean = jnp.sum(total, axis=1, keepdims=True) / (blocks * feats)
    spread = jnp.zeros((rows, 128), f32)
    for p in range(blocks):
        centred = x_ref[p].astype(f32) - mean
        square = centred * centred
        for j in range(0, feats, 128):
            spread += square[:, j : j + 128]
        scaled = (centred * gain_ref[(first + p) % blocks, core]).astype(bf16)
        for copy in w_copies[p]:
            copy.wait()
        term = jnp.dot(scaled, weight_ref[p], preferred_element_type=f32)
        if p == 0:
            q_ref[:, :width] = term
        else:
            q_ref[:, :width] += term
    spread = jnp.sum(spread, axis=1, keepdims=True) / (blocks * feats)
    lane = lax.broadcasted_iota(jnp.int32, (rows, 128), 1)
    q_ref[:, width:] = jnp.where(lane == 0, mean, spread)


def forward(place, near, far, gain, weight, other):
    _, rows, feats = near.shape
    blocks, _, width = other.shape
    return pl.pallas_call(
        forward_kernel,
        in_specs=[SCALAR, ANYWHERE, ANYWHERE] + in_vmem(1) + [ANYWHERE, ANYWHERE],
        out_specs=in_vmem(1)[0],
        out_shape=jax.ShapeDtypeStruct((rows, 2 * width + 128), f32),
        scratch_shapes=[
            pltpu.VMEM((blocks, rows, feats), bf16),
            pltpu.VMEM((blocks, feats, 2 * width), bf16),
            pltpu.SemaphoreType.DMA((blocks,)),
            pltpu.SemaphoreType.DMA((blocks,)),
            pltpu.SemaphoreType.DMA((blocks,)),
        ],
        compiler_params=PARAMS,
        name="forward",
    )(place, near, far, gain, weight, other)


def split_sums(first, second):
    rows = first.shape[0]
    lane = lax.broadcasted_iota(jnp.int32, (rows, 128), 1)
    value = jnp.where(lane < 2, first, second)
    high = value.astype(bf16).astype(f32)
    return jnp.where(lane % 2 == 0, high, value - high).T[:PAD]


def backward_kernel(
    place_ref,
    q_ref,
    got_ref,
    up_ref,
    upo_ref,
    vec_ref,
    veco_ref,
    weight_any,
    other_any,
    p_any,
    pg_ref,
    st_ref,
    weight_ref,
    p_ref,
    w_sem,
    o_sem,
    p_sem,
):
    half, feats, width = weight_ref.shape
    width = width // 2
    rows = q_ref.shape[0]
    core, first = place_ref[0], place_ref[1]
    w_copies = weight_copies(core, first + half, weight_any, other_any, weight_ref, w_sem, o_sem)
    p_copies = [pltpu.make_async_copy(p_ref.at[p], p_any.at[p], p_sem.at[p]) for p in range(half)]
    for pair in w_copies:
        for copy in pair:
            copy.start()
    mine, theirs = q_ref[:, 2 * width :], got_ref[:, 2 * width :]
    mean_here, mean_there = mine[:, 0:1], theirs[:, 0:1]
    gap = 0.5 * (mean_here - mean_there)
    mean = 0.5 * (mean_here + mean_there)
    variance = 0.5 * (mine[:, 1:2] + theirs[:, 1:2]) + gap * gap
    inv_std = lax.rsqrt(variance + epsilon)
    lane = lax.broadcasted_iota(jnp.int32, (rows, 128), 1)
    st_ref[...] = jnp.where(lane == 0, mean, inv_std)
    gap = gap * jnp.where(core == 0, 1.0, -1.0)

    def grad(summed, up, vec):
        raw = inv_std * (summed + gap * (vec[1:2, :] - vec[2:3, :]))
        preact = raw + vec[0:1, :]
        gate = 1.0 / (1.0 + jnp.exp(-preact))
        pg = (up.astype(f32) * gate * (1.0 + preact * (1.0 - gate))).astype(bf16)
        wide = pg.astype(f32)
        scale = vec[1:2, :] + vec[2:3, :]
        return (
            pg,
            jnp.sum(wide * scale, axis=1, keepdims=True),
            jnp.sum(wide * raw, axis=1, keepdims=True),
        )

    pg, sum_g, sum_gu = grad(q_ref[:, :width] + got_ref[:, width : 2 * width], up_ref[...], vec_ref[...])
    pgo, sum_go, sum_guo = grad(
        q_ref[:, width : 2 * width] + got_ref[:, :width], upo_ref[...], veco_ref[...]
    )
    both = jnp.concatenate([pg, pgo], axis=1)
    pg_ref[...] = both
    tail = split_sums(sum_g + sum_go, sum_gu + sum_guo).astype(bf16)
    tail = jnp.concatenate([tail, jnp.zeros((PAD, feats - rows), bf16)], axis=1)
    for p in range(half):
        for copy in w_copies[p]:
            copy.wait()
        p_ref[p, :rows] = lax.dot_general(both, weight_ref[p], NT, preferred_element_type=f32).astype(bf16)
        p_ref[p, rows:] = tail
        p_copies[p].start()
    for copy in p_copies:
        copy.wait()


def backward(place, q, got, up, upo, vec, veco, weight, other):
    blocks, feats, width = other.shape
    rows, half = q.shape[0], blocks // 2
    return pl.pallas_call(
        backward_kernel,
        in_specs=[SCALAR] + in_vmem(6) + [ANYWHERE, ANYWHERE],
        out_specs=[ANYWHERE] + in_vmem(2),
        out_shape=[
            pltpu.HBM((half, rows + PAD, feats), bf16),
            pltpu.HBM((rows, 2 * width), bf16),
            jax.ShapeDtypeStruct((rows, 128), f32),
        ],
        scratch_shapes=[
            pltpu.VMEM((half, feats, 2 * width), bf16),
            pltpu.VMEM((half, rows + PAD, feats), bf16),
            pltpu.SemaphoreType.DMA((half,)),
            pltpu.SemaphoreType.DMA((half,)),
            pltpu.SemaphoreType.DMA((half,)),
        ],
        compiler_params=PARAMS,
        name="backward",
    )(place, q, got, up, upo, vec, veco, weight, other)


def second_kernel(place_ref, pg_ref, weight_any, other_any, p_any, weight_ref, p_ref, w_sem, o_sem, p_sem):
    half = p_ref.shape[0]
    core, first = place_ref[0], place_ref[1]
    w_copies = weight_copies(core, first, weight_any, other_any, weight_ref, w_sem, o_sem)
    p_copies = [pltpu.make_async_copy(p_ref.at[p], p_any.at[p], p_sem.at[p]) for p in range(half)]
    for pair in w_copies:
        for copy in pair:
            copy.start()
    both = pg_ref[...]
    for p in range(half):
        for copy in w_copies[p]:
            copy.wait()
        p_ref[p] = lax.dot_general(both, weight_ref[p], NT, preferred_element_type=f32).astype(bf16)
        p_copies[p].start()
    for copy in p_copies:
        copy.wait()


def second(place, pg, weight, other):
    blocks, feats, width = other.shape
    rows, half = pg.shape[0], blocks // 2
    return pl.pallas_call(
        second_kernel,
        in_specs=[SCALAR] + in_vmem(1) + [ANYWHERE, ANYWHERE],
        out_specs=ANYWHERE,
        out_shape=pltpu.HBM((half, rows, feats), bf16),
        scratch_shapes=[
            pltpu.VMEM((half, feats, 2 * width), bf16),
            pltpu.VMEM((half, rows, feats), bf16),
            pltpu.SemaphoreType.DMA((half,)),
            pltpu.SemaphoreType.DMA((half,)),
            pltpu.SemaphoreType.DMA((half,)),
        ],
        compiler_params=PARAMS,
        name="second",
    )(place, pg, weight, other)


def gather_sums(tail):
    sums = tail.T
    return sums[:, 0:1] + sums[:, 1:2], sums[:, 2:3] + sums[:, 3:4]


def meet_kernel(part_any, sum_ref, own_ref, part_ref, sem):
    blocks, padded, feats = part_ref.shape
    rows = padded - PAD
    copies = [pltpu.make_async_copy(part_any.at[p], part_ref.at[p], sem.at[p]) for p in range(blocks)]
    for copy in copies:
        copy.start()
    copies[0].wait()
    total = part_ref[0].astype(f32)
    for p in range(1, blocks):
        copies[p].wait()
        total += part_ref[p].astype(f32)
    sum_g, sum_gu = gather_sums(total[rows : rows + 8, :rows])
    lane = lax.broadcasted_iota(jnp.int32, (rows, 128), 1)
    own_ref[...] = jnp.where(lane == 0, sum_g, sum_gu)
    sum_ref[:rows] = total[:rows].astype(bf16)
    tail = split_sums(sum_g, sum_gu).astype(bf16)
    sum_ref[rows:] = jnp.concatenate([tail, jnp.zeros((PAD, feats - rows), bf16)], axis=1)


def meet(part):
    blocks, padded, feats = part.shape
    return pl.pallas_call(
        meet_kernel,
        in_specs=[ANYWHERE],
        out_specs=in_vmem(2),
        out_shape=[pltpu.VMEM((padded, feats), bf16), pltpu.VMEM((padded - PAD, 128), f32)],
        scratch_shapes=[pltpu.VMEM(part.shape, bf16), pltpu.SemaphoreType.DMA((blocks,))],
        compiler_params=PARAMS,
        name="meet",
    )(part)


def finish_kernel(back_ref, across_ref, own_ref, x_ref, st_ref, gain_ref, target_ref, slot_ref, send_ref):
    blocks, rows, feats = back_ref.shape
    owners = send_ref.shape[0]
    total = across_ref[:rows].astype(f32)
    for p in range(blocks):
        total += back_ref[p].astype(f32)
    sum_g, sum_gu = gather_sums(across_ref[rows:, :rows].astype(f32)[:8])
    count = 4 * blocks * feats
    mean_g = (sum_g + own_ref[:, 0:1]) / count
    mean_gu = (sum_gu + own_ref[:, 1:2]) / count
    mean, inv_std = st_ref[:, 0:1], st_ref[:, 1:2]
    unit = (x_ref[...].astype(f32) - mean) * inv_std
    grad = (inv_std * (total * gain_ref[...] - mean_g - unit * mean_gu)).astype(bf16)
    slots = owners * CAPACITY
    placing = lax.broadcasted_iota(jnp.int32, (slots, rows), 0) == target_ref[...]
    placed = jnp.dot(
        jnp.where(placing, 1.0, 0.0).astype(bf16), grad, preferred_element_type=f32
    ).astype(bf16)
    placed = placed.reshape(owners, CAPACITY, feats)
    for k in range(feats // 128):
        send_ref[:, k * CAPACITY : (k + 1) * CAPACITY, :] = placed[:, :, k * 128 : (k + 1) * 128]
    send_ref[:, feats // 128 * CAPACITY :, :] = jnp.broadcast_to(
        slot_ref[...][:, None, :], (owners, 8, 128)
    )


def finish(back, across, own, x, st, gain, target, slot):
    owners = slot.shape[0]
    return pl.pallas_call(
        finish_kernel,
        in_specs=in_vmem(8),
        out_specs=in_vmem(1)[0],
        out_shape=pltpu.VMEM((owners, x.shape[1] // 128 * CAPACITY + 8, 128), bf16),
        compiler_params=PARAMS,
        name="finish",
    )(*held(back, across, own, x, st, gain, target, slot))


def landing_kernel(got_ref, o_ref):
    rows, feats = o_ref.shape
    owners = got_ref.shape[0]
    slots = owners * CAPACITY
    pieces = feats // 128
    held_slots = got_ref[:, pieces * CAPACITY, :].astype(bf16)
    spread = lax.broadcasted_iota(jnp.int32, (128, slots), 0) == (
        lax.broadcasted_iota(jnp.int32, (128, slots), 1) % CAPACITY
    )
    every = jnp.dot(held_slots, jnp.where(spread, 1.0, 0.0).astype(bf16), preferred_element_type=f32)
    own = lax.broadcasted_iota(jnp.int32, (owners, slots), 0) == (
        lax.broadcasted_iota(jnp.int32, (owners, slots), 1) // CAPACITY
    )
    slot = jnp.sum(jnp.where(own, every, 0.0), axis=0, keepdims=True).astype(jnp.int32)
    landing = lax.broadcasted_iota(jnp.int32, (rows, slots), 0) == slot
    landing = jnp.where(landing, 1.0, 0.0).astype(bf16)
    for k in range(pieces):
        piece = got_ref[:, k * CAPACITY : (k + 1) * CAPACITY, :].reshape(slots, 128)
        o_ref[:, k * 128 : (k + 1) * 128] = jnp.dot(
            landing, piece, preferred_element_type=f32
        ).astype(bf16)


def land(got, rows, feats):
    return pl.pallas_call(
        landing_kernel,
        in_specs=in_vmem(1),
        out_specs=in_vmem(1)[0],
        out_shape=jax.ShapeDtypeStruct((rows, feats), bf16),
        compiler_params=PARAMS,
        name="land",
    )(*held(got))


def per_device(inputs, upstream, proj_weight, proj_bias, norm_gain, home_rows):
    rows, feats = inputs.shape
    width = upstream.shape[1]
    n_tensor, owners = lax.axis_size("tensor"), lax.axis_size("dp")
    chips = n_tensor // 2
    side = chips // 2
    me = lax.axis_index("tensor")
    core, first = me % 2, me // (2 * side) * side
    swap = [(t, t ^ 1) for t in range(n_tensor)]
    cross = [(t, (t + 2 * side) % n_tensor) for t in range(n_tensor)]
    lines = [[2 * side * h + 2 * k + c for k in range(side)] for h in range(2) for c in range(2)]
    place = jnp.stack([core, first]).astype(jnp.int32)

    def exchange(blocks):
        return lax.all_to_all(blocks, "tensor", 0, 0, axis_index_groups=lines, tiled=True)

    facing = lax.ppermute(inputs, "tensor", cross)
    near = exchange(jnp.broadcast_to(inputs[None], (side, rows, feats)))
    far = exchange(jnp.broadcast_to(facing[None], (side, rows, feats)))

    pairs = proj_weight.reshape(chips, 2, feats, width)
    cut = lax.dynamic_index_in_dim(pairs, 1 - core, 1, False)
    other = lax.ppermute(cut, "tensor", swap)
    upo = lax.ppermute(upstream, "tensor", swap)
    gains = norm_gain.reshape(chips, 2, 1, feats)
    scales = jnp.sum(norm_gain.reshape(chips, 2, feats, 1) * pairs.astype(f32), axis=(0, 2))
    vec = jnp.concatenate([proj_bias[None], scales], axis=0)
    veco = lax.ppermute(vec, "tensor", swap)

    owner_of = home_rows // rows
    home_slot = home_rows % rows
    order_ids = jnp.arange(rows, dtype=jnp.int32)
    earlier = jnp.sum(
        ((owner_of[:, None] == owner_of[None, :]) & (order_ids[:, None] > order_ids[None, :])).astype(
            jnp.int32
        ),
        axis=1,
    )
    target = owner_of * CAPACITY + earlier
    lanes = jnp.arange(128, dtype=jnp.int32)
    held_at = (jnp.arange(owners, dtype=jnp.int32)[:, None] * CAPACITY + lanes[None, :])[:, :, None]
    match = (held_at == target[None, None, :]) & (lanes < CAPACITY)[None, :, None]
    slot = jnp.sum(jnp.where(match, home_slot[None, None, :] + 1, 0), axis=2) - 1
    slot = slot.astype(f32).astype(bf16)

    own_gain = lax.dynamic_index_in_dim(norm_gain.reshape(n_tensor, 1, feats), me, 0, False)
    near, far, other, upo, veco, slot, target, own_gain = lax.optimization_barrier(
        (near, far, other, upo, veco, slot, target, own_gain)
    )
    q = forward(place, near, far, gains, pairs, other)
    got = lax.ppermute(q, "tensor", swap)
    away, pg, st = backward(place, q, got, upstream, upo, vec, veco, pairs, other)
    met = exchange(away)
    home = second(place, pg, pairs, other)
    summed, own = meet(met)
    across = lax.ppermute(summed, "tensor", cross)
    back = exchange(home)
    send = finish(back, across, own, inputs, st, own_gain, target[None, :], slot)
    arrived = lax.all_to_all(send, "dp", split_axis=0, concat_axis=0, tiled=True)
    return land(arrived, rows, feats)


def solution(mesh):
    return jax.shard_map(
        per_device,
        mesh=mesh,
        in_specs=(
            P("dp", "tensor"),
            P("dp", "tensor"),
            P(None, "tensor"),
            P("tensor"),
            P(),
            P("dp"),
        ),
        out_specs=P("dp", "tensor"),
        check_vma=False,
    )
```

```python
import jax
import jax.numpy as jnp
from jax import lax
from jax.experimental import pallas as pl
from jax.experimental.pallas import tpu as pltpu
from jax.sharding import PartitionSpec as P


epsilon = 1e-05
f32, bf16 = jnp.float32, jnp.bfloat16
PAD = 16
CAPACITY = 16
NT = (((1,), (1,)), ((), ()))


def in_vmem(n):
    return [pl.BlockSpec(memory_space=pltpu.VMEM) for _ in range(n)]


def held(*arrays):
    return [pltpu.with_memory_space_constraint(a, pltpu.VMEM) for a in arrays]


PARAMS = pltpu.CompilerParams(vmem_limit_bytes=16 * 1024 * 1024)


ANYWHERE = pl.BlockSpec(memory_space=pl.ANY)
SCALAR = pl.BlockSpec(memory_space=pltpu.SMEM)


def spread_kernel(x_ref, o_any, sem):
    copies = [pltpu.make_async_copy(x_ref, o_any.at[b], sem.at[b]) for b in range(o_any.shape[0])]
    for copy in copies:
        copy.start()
    for copy in copies:
        copy.wait()


def spread(x, blocks):
    return pl.pallas_call(
        spread_kernel,
        in_specs=in_vmem(1),
        out_specs=ANYWHERE,
        out_shape=pltpu.HBM((blocks,) + x.shape, x.dtype),
        scratch_shapes=[pltpu.SemaphoreType.DMA((blocks,))],
        compiler_params=PARAMS,
        name="spread",
    )(x)


def weight_copies(core, weight_any, other_any, weight_ref, w_sem, o_sem):
    blocks, _, width = weight_ref.shape
    half = width // 2
    return [
        (
            pltpu.make_async_copy(weight_any.at[b, core], weight_ref.at[b, :, :half], w_sem.at[b]),
            pltpu.make_async_copy(other_any.at[b], weight_ref.at[b, :, half:], o_sem.at[b]),
        )
        for b in range(blocks)
    ]


def forward_kernel(
    core_ref, x_any, gain_ref, weight_any, other_any, q_ref, x_ref, weight_ref, x_sem, w_sem, o_sem
):
    blocks, rows, feats = x_ref.shape
    width = weight_ref.shape[2]
    core = core_ref[0]
    x_copies = [pltpu.make_async_copy(x_any.at[b], x_ref.at[b], x_sem.at[b]) for b in range(blocks)]
    w_copies = weight_copies(core, weight_any, other_any, weight_ref, w_sem, o_sem)
    for b in range(blocks):
        x_copies[b].start()
        for copy in w_copies[b]:
            copy.start()
    x_copies[0].wait()
    pivot = jnp.mean(x_ref[0].astype(f32), axis=1, keepdims=True)
    total = jnp.zeros((rows, 128), f32)
    square = jnp.zeros((rows, 128), f32)
    for b in range(blocks):
        if b > 0:
            x_copies[b].wait()
        moved = x_ref[b].astype(f32) - pivot
        for j in range(0, feats, 128):
            part = moved[:, j : j + 128]
            total += part
            square += part * part
        scaled = (moved * gain_ref[b, core]).astype(bf16)
        for copy in w_copies[b]:
            copy.wait()
        term = jnp.dot(scaled, weight_ref[b], preferred_element_type=f32)
        if b == 0:
            q_ref[:, :width] = term
        else:
            q_ref[:, :width] += term
    shift = jnp.sum(total, axis=1, keepdims=True) / (blocks * feats)
    spread = jnp.sum(square, axis=1, keepdims=True) / (blocks * feats) - shift * shift
    lane = lax.broadcasted_iota(jnp.int32, (rows, 128), 1)
    q_ref[:, width:] = jnp.where(
        lane == 0, pivot, jnp.where(lane == 1, pivot + shift, jnp.maximum(spread, 0.0))
    )


def forward(core, x, gain, weight, other):
    blocks, rows, feats = x.shape
    width = other.shape[2]
    return pl.pallas_call(
        forward_kernel,
        in_specs=[SCALAR, ANYWHERE] + in_vmem(1) + [ANYWHERE, ANYWHERE],
        out_specs=in_vmem(1)[0],
        out_shape=jax.ShapeDtypeStruct((rows, 2 * width + 128), f32),
        scratch_shapes=[
            pltpu.VMEM(x.shape, bf16),
            pltpu.VMEM((blocks, feats, 2 * width), bf16),
            pltpu.SemaphoreType.DMA((blocks,)),
            pltpu.SemaphoreType.DMA((blocks,)),
            pltpu.SemaphoreType.DMA((blocks,)),
        ],
        compiler_params=PARAMS,
        name="forward",
    )(core, x, gain, weight, other)


def backward_kernel(
    core_ref,
    q_ref,
    got_ref,
    up_ref,
    upo_ref,
    vec_ref,
    veco_ref,
    weight_any,
    other_any,
    p_ref,
    st_ref,
    weight_ref,
    w_sem,
    o_sem,
):
    blocks, feats, width = weight_ref.shape
    width = width // 2
    rows = q_ref.shape[0]
    core = core_ref[0]
    w_copies = weight_copies(core, weight_any, other_any, weight_ref, w_sem, o_sem)
    for pair in w_copies:
        for copy in pair:
            copy.start()
    mine, theirs = q_ref[:, 2 * width :], got_ref[:, 2 * width :]
    gap = 0.5 * (mine[:, 1:2] - theirs[:, 1:2])
    mean = 0.5 * (mine[:, 1:2] + theirs[:, 1:2])
    variance = 0.5 * (mine[:, 2:3] + theirs[:, 2:3]) + gap * gap
    inv_std = lax.rsqrt(variance + epsilon)
    lane = lax.broadcasted_iota(jnp.int32, (rows, 128), 1)
    st_ref[...] = jnp.where(lane == 0, mean, inv_std)
    even = jnp.where(core == 0, mine[:, 0:1], theirs[:, 0:1]) - mean
    odd = jnp.where(core == 0, theirs[:, 0:1], mine[:, 0:1]) - mean

    def grad(summed, up, vec):
        raw = inv_std * (summed + even * vec[1:2, :] + odd * vec[2:3, :])
        preact = raw + vec[0:1, :]
        gate = 1.0 / (1.0 + jnp.exp(-preact))
        pg = (up.astype(f32) * gate * (1.0 + preact * (1.0 - gate))).astype(bf16)
        wide = pg.astype(f32)
        scale = vec[1:2, :] + vec[2:3, :]
        return (
            pg,
            jnp.sum(wide * scale, axis=1, keepdims=True),
            jnp.sum(wide * raw, axis=1, keepdims=True),
        )

    pg, sum_g, sum_gu = grad(q_ref[:, :width] + got_ref[:, width : 2 * width], up_ref[...], vec_ref[...])
    pgo, sum_go, sum_guo = grad(
        q_ref[:, width : 2 * width] + got_ref[:, :width], upo_ref[...], veco_ref[...]
    )
    both = jnp.concatenate([pg, pgo], axis=1)
    value = jnp.where(lane < 2, sum_g + sum_go, sum_gu + sum_guo)
    high = value.astype(bf16).astype(f32)
    tail = jnp.where(lane % 2 == 0, high, value - high).T[:PAD].astype(bf16)
    tail = jnp.concatenate([tail, jnp.zeros((PAD, feats - rows), bf16)], axis=1)
    for b in range(blocks):
        for copy in w_copies[b]:
            copy.wait()
        p_ref[b, :rows] = lax.dot_general(both, weight_ref[b], NT, preferred_element_type=f32).astype(bf16)
        p_ref[b, rows:] = tail


def backward(core, q, got, up, upo, vec, veco, weight, other):
    blocks, feats, width = other.shape
    rows = q.shape[0]
    return pl.pallas_call(
        backward_kernel,
        in_specs=[SCALAR] + in_vmem(6) + [ANYWHERE, ANYWHERE],
        out_specs=in_vmem(2),
        out_shape=[
            pltpu.VMEM((blocks, rows + PAD, feats), bf16),
            pltpu.VMEM((rows, 128), f32),
        ],
        scratch_shapes=[
            pltpu.VMEM((blocks, feats, 2 * width), bf16),
            pltpu.SemaphoreType.DMA((blocks,)),
            pltpu.SemaphoreType.DMA((blocks,)),
        ],
        compiler_params=PARAMS,
        name="backward",
    )(core, q, got, up, upo, vec, veco, weight, other)


def finish_kernel(back_ref, x_ref, st_ref, gain_ref, target_ref, slot_ref, send_ref):
    blocks = back_ref.shape[0]
    rows, feats = x_ref.shape
    owners = send_ref.shape[0]
    total = back_ref[0].astype(f32)
    for b in range(1, blocks):
        total += back_ref[b].astype(f32)
    tail = total[rows : rows + 8, :rows]
    sums = tail.T / (2 * blocks * feats)
    first = sums[:, 0:1] + sums[:, 1:2]
    second = sums[:, 2:3] + sums[:, 3:4]
    mean, inv_std = st_ref[:, 0:1], st_ref[:, 1:2]
    unit = (x_ref[...].astype(f32) - mean) * inv_std
    grad = (inv_std * (total[:rows] * gain_ref[...] - first - unit * second)).astype(bf16)
    slots = owners * CAPACITY
    placing = lax.broadcasted_iota(jnp.int32, (slots, rows), 0) == target_ref[...]
    placed = jnp.dot(
        jnp.where(placing, 1.0, 0.0).astype(bf16), grad, preferred_element_type=f32
    ).astype(bf16)
    placed = placed.reshape(owners, CAPACITY, feats)
    for k in range(feats // 128):
        send_ref[:, k * CAPACITY : (k + 1) * CAPACITY, :] = placed[:, :, k * 128 : (k + 1) * 128]
    send_ref[:, feats // 128 * CAPACITY :, :] = jnp.broadcast_to(slot_ref[...][:, None, :], (owners, 8, 128))


def finish(back, x, st, gain, target, slot):
    owners = slot.shape[0]
    return pl.pallas_call(
        finish_kernel,
        in_specs=in_vmem(6),
        out_specs=in_vmem(1)[0],
        out_shape=pltpu.VMEM((owners, x.shape[1] // 128 * CAPACITY + 8, 128), bf16),
        compiler_params=PARAMS,
        name="finish",
    )(*held(back, x, st, gain, target, slot))


def landing_kernel(got_ref, o_ref):
    rows, feats = o_ref.shape
    owners = got_ref.shape[0]
    slots = owners * CAPACITY
    pieces = feats // 128
    held_slots = got_ref[:, pieces * CAPACITY, :].astype(bf16)
    spread = lax.broadcasted_iota(jnp.int32, (128, slots), 0) == (
        lax.broadcasted_iota(jnp.int32, (128, slots), 1) % CAPACITY
    )
    every = jnp.dot(held_slots, jnp.where(spread, 1.0, 0.0).astype(bf16), preferred_element_type=f32)
    own = lax.broadcasted_iota(jnp.int32, (owners, slots), 0) == (
        lax.broadcasted_iota(jnp.int32, (owners, slots), 1) // CAPACITY
    )
    slot = jnp.sum(jnp.where(own, every, 0.0), axis=0, keepdims=True).astype(jnp.int32)
    landing = lax.broadcasted_iota(jnp.int32, (rows, slots), 0) == slot
    landing = jnp.where(landing, 1.0, 0.0).astype(bf16)
    for k in range(pieces):
        piece = got_ref[:, k * CAPACITY : (k + 1) * CAPACITY, :].reshape(slots, 128)
        o_ref[:, k * 128 : (k + 1) * 128] = jnp.dot(
            landing, piece, preferred_element_type=f32
        ).astype(bf16)


def land(got, rows, feats):
    return pl.pallas_call(
        landing_kernel,
        in_specs=in_vmem(1),
        out_specs=in_vmem(1)[0],
        out_shape=jax.ShapeDtypeStruct((rows, feats), bf16),
        compiler_params=PARAMS,
        name="land",
    )(*held(got))


def per_device(inputs, upstream, proj_weight, proj_bias, norm_gain, home_rows):
    rows, feats = inputs.shape
    width = upstream.shape[1]
    n_tensor, owners = lax.axis_size("tensor"), lax.axis_size("dp")
    chips = n_tensor // 2
    me = lax.axis_index("tensor")
    core = me % 2
    swap = [(t, t ^ 1) for t in range(n_tensor)]
    classes = [[2 * k + c for k in range(chips)] for c in range(2)]
    core_arr = core.reshape(1).astype(jnp.int32)

    sent = spread(inputs, chips)
    half = lax.all_to_all(sent, "tensor", 0, 0, axis_index_groups=classes, tiled=True)

    pairs = proj_weight.reshape(chips, 2, feats, width)
    cut = lax.dynamic_index_in_dim(pairs, 1 - core, 1, False)
    other = lax.ppermute(cut, "tensor", swap)
    upo = lax.ppermute(upstream, "tensor", swap)
    gains = norm_gain.reshape(chips, 2, 1, feats)
    scales = jnp.sum(norm_gain.reshape(chips, 2, feats, 1) * pairs.astype(f32), axis=(0, 2))
    vec = jnp.concatenate([proj_bias[None], scales], axis=0)
    veco = lax.ppermute(vec, "tensor", swap)

    owner_of = home_rows // rows
    home_slot = home_rows % rows
    order_ids = jnp.arange(rows, dtype=jnp.int32)
    earlier = jnp.sum(
        ((owner_of[:, None] == owner_of[None, :]) & (order_ids[:, None] > order_ids[None, :])).astype(
            jnp.int32
        ),
        axis=1,
    )
    target = owner_of * CAPACITY + earlier
    lanes = jnp.arange(128, dtype=jnp.int32)
    held_at = (jnp.arange(owners, dtype=jnp.int32)[:, None] * CAPACITY + lanes[None, :])[:, :, None]
    match = (held_at == target[None, None, :]) & (lanes < CAPACITY)[None, :, None]
    slot = jnp.sum(jnp.where(match, home_slot[None, None, :] + 1, 0), axis=2) - 1
    slot = slot.astype(f32).astype(bf16)

    own_gain = lax.dynamic_index_in_dim(norm_gain.reshape(n_tensor, 1, feats), me, 0, False)
    half, other, upo, veco, slot, target, own_gain = lax.optimization_barrier(
        (half, other, upo, veco, slot, target, own_gain)
    )
    q = forward(core_arr, half, gains, pairs, other)
    got = lax.ppermute(q, "tensor", swap)
    parts, st = backward(core_arr, q, got, upstream, upo, vec, veco, pairs, other)
    back = lax.all_to_all(parts, "tensor", 0, 0, axis_index_groups=classes, tiled=True)
    send = finish(back, inputs, st, own_gain, target[None, :], slot)
    arrived = lax.all_to_all(send, "dp", split_axis=0, concat_axis=0, tiled=True)
    return land(arrived, rows, feats)


def solution(mesh):
    return jax.shard_map(
        per_device,
        mesh=mesh,
        in_specs=(
            P("dp", "tensor"),
            P("dp", "tensor"),
            P(None, "tensor"),
            P("tensor"),
            P(),
            P("dp"),
        ),
        out_specs=P("dp", "tensor"),
        check_vma=False,
    )
```

```python
import jax
import jax.numpy as jnp
from jax import lax
from jax.experimental import pallas as pl
from jax.experimental.pallas import tpu as pltpu
from jax.sharding import PartitionSpec as P


epsilon = 1e-05
f32, bf16 = jnp.float32, jnp.bfloat16
PAD = 8
CAPACITY = 16
NT = (((1,), (1,)), ((), ()))


def in_vmem(n):
    return [pl.BlockSpec(memory_space=pltpu.VMEM) for _ in range(n)]


def held(*arrays):
    return [pltpu.with_memory_space_constraint(a, pltpu.VMEM) for a in arrays]


PARAMS = pltpu.CompilerParams(vmem_limit_bytes=16 * 1024 * 1024)


ANYWHERE = pl.BlockSpec(memory_space=pl.ANY)
SCALAR = pl.BlockSpec(memory_space=pltpu.SMEM)


def spread_kernel(x_any, o_any, sem):
    copies = [pltpu.make_async_copy(x_any, o_any.at[b], sem.at[b]) for b in range(o_any.shape[0])]
    for copy in copies:
        copy.start()
    for copy in copies:
        copy.wait()


def spread(x, blocks):
    return pl.pallas_call(
        spread_kernel,
        in_specs=[ANYWHERE],
        out_specs=ANYWHERE,
        out_shape=pltpu.HBM((blocks,) + x.shape, x.dtype),
        scratch_shapes=[pltpu.SemaphoreType.DMA((blocks,))],
        compiler_params=PARAMS,
        name="spread",
    )(pltpu.with_memory_space_constraint(x, pltpu.HBM))


def weight_copies(core, weight_any, other_any, weight_ref, w_sem, o_sem):
    blocks, _, width = weight_ref.shape
    half = width // 2
    return [
        (
            pltpu.make_async_copy(weight_any.at[b, core], weight_ref.at[b, :, :half], w_sem.at[b]),
            pltpu.make_async_copy(other_any.at[b], weight_ref.at[b, :, half:], o_sem.at[b]),
        )
        for b in range(blocks)
    ]


def forward_kernel(
    core_ref, x_any, gain_ref, weight_any, other_any, q_ref, x_ref, weight_ref, rows_ref, x_sem, w_sem, o_sem
):
    blocks, rows, feats = x_ref.shape
    width = weight_ref.shape[2]
    core = core_ref[0]
    x_copies = [pltpu.make_async_copy(x_any.at[b], x_ref.at[b], x_sem.at[b]) for b in range(blocks)]
    w_copies = weight_copies(core, weight_any, other_any, weight_ref, w_sem, o_sem)
    for b in range(blocks):
        x_copies[b].start()
        for copy in w_copies[b]:
            copy.start()
    x_copies[0].wait()
    pivot = jnp.mean(x_ref[0].astype(f32), axis=1, keepdims=True)
    total = jnp.zeros((rows, 128), f32)
    square = jnp.zeros((rows, 128), f32)
    for b in range(blocks):
        if b > 0:
            x_copies[b].wait()
        moved = x_ref[b].astype(f32) - pivot
        for j in range(0, feats, 128):
            part = moved[:, j : j + 128]
            total += part
            square += part * part
        rows_ref[:, b * feats : (b + 1) * feats] = (moved * gain_ref[b, core]).astype(bf16)
        for copy in w_copies[b]:
            copy.wait()
    q_ref[:, :width] = jnp.dot(
        rows_ref[...], weight_ref[...].reshape(blocks * feats, width), preferred_element_type=f32
    )
    shift = jnp.sum(total, axis=1, keepdims=True) / (blocks * feats)
    spread = jnp.sum(square, axis=1, keepdims=True) / (blocks * feats) - shift * shift
    lane = lax.broadcasted_iota(jnp.int32, (rows, 128), 1)
    q_ref[:, width:] = jnp.where(
        lane == 0, pivot, jnp.where(lane == 1, pivot + shift, jnp.maximum(spread, 0.0))
    )


def forward(core, x, gain, weight, other):
    blocks, rows, feats = x.shape
    width = other.shape[2]
    return pl.pallas_call(
        forward_kernel,
        in_specs=[SCALAR, ANYWHERE] + in_vmem(1) + [ANYWHERE, ANYWHERE],
        out_specs=in_vmem(1)[0],
        out_shape=jax.ShapeDtypeStruct((rows, 2 * width + 128), f32),
        scratch_shapes=[
            pltpu.VMEM(x.shape, bf16),
            pltpu.VMEM((blocks, feats, 2 * width), bf16),
            pltpu.VMEM((rows, blocks * feats), bf16),
            pltpu.SemaphoreType.DMA((blocks,)),
            pltpu.SemaphoreType.DMA((blocks,)),
            pltpu.SemaphoreType.DMA((blocks,)),
        ],
        compiler_params=PARAMS,
        name="forward",
    )(core, x, gain, weight, other)


def backward_kernel(
    core_ref,
    q_ref,
    got_ref,
    up_ref,
    upo_ref,
    vec_ref,
    veco_ref,
    weight_any,
    other_any,
    p_ref,
    st_ref,
    weight_ref,
    w_sem,
    o_sem,
):
    blocks, feats, width = weight_ref.shape
    width = width // 2
    rows = q_ref.shape[0]
    core = core_ref[0]
    w_copies = weight_copies(core, weight_any, other_any, weight_ref, w_sem, o_sem)
    for pair in w_copies:
        for copy in pair:
            copy.start()
    mine, theirs = q_ref[:, 2 * width :], got_ref[:, 2 * width :]
    gap = 0.5 * (mine[:, 1:2] - theirs[:, 1:2])
    mean = 0.5 * (mine[:, 1:2] + theirs[:, 1:2])
    variance = 0.5 * (mine[:, 2:3] + theirs[:, 2:3]) + gap * gap
    inv_std = lax.rsqrt(variance + epsilon)
    lane = lax.broadcasted_iota(jnp.int32, (rows, 128), 1)
    st_ref[...] = jnp.where(lane == 0, mean, inv_std)
    even = jnp.where(core == 0, mine[:, 0:1], theirs[:, 0:1]) - mean
    odd = jnp.where(core == 0, theirs[:, 0:1], mine[:, 0:1]) - mean

    def grad(summed, up, vec):
        raw = inv_std * (summed + even * vec[1:2, :] + odd * vec[2:3, :])
        preact = raw + vec[0:1, :]
        gate = 1.0 / (1.0 + jnp.exp(-preact))
        pg = (up.astype(f32) * gate * (1.0 + preact * (1.0 - gate))).astype(bf16)
        wide = pg.astype(f32)
        scale = vec[1:2, :] + vec[2:3, :]
        return (
            pg,
            jnp.sum(wide * scale, axis=1, keepdims=True),
            jnp.sum(wide * raw, axis=1, keepdims=True),
        )

    pg, sum_g, sum_gu = grad(q_ref[:, :width] + got_ref[:, width : 2 * width], up_ref[...], vec_ref[...])
    pgo, sum_go, sum_guo = grad(
        q_ref[:, width : 2 * width] + got_ref[:, :width], upo_ref[...], veco_ref[...]
    )
    both = jnp.concatenate([pg, pgo], axis=1)
    value = jnp.where(lane < 2, sum_g + sum_go, sum_gu + sum_guo)
    high = value.astype(bf16).astype(f32)
    tail = jnp.where(lane % 2 == 0, high, value - high).T[:PAD].astype(bf16)
    tail = jnp.concatenate([tail, jnp.zeros((PAD, feats - rows), bf16)], axis=1)
    for b in range(blocks):
        for copy in w_copies[b]:
            copy.wait()
        p_ref[b, :rows] = lax.dot_general(both, weight_ref[b], NT, preferred_element_type=f32).astype(bf16)
        p_ref[b, rows:] = tail


def backward(core, q, got, up, upo, vec, veco, weight, other):
    blocks, feats, width = other.shape
    rows = q.shape[0]
    return pl.pallas_call(
        backward_kernel,
        in_specs=[SCALAR] + in_vmem(6) + [ANYWHERE, ANYWHERE],
        out_specs=in_vmem(2),
        out_shape=[
            pltpu.VMEM((blocks, rows + PAD, feats), bf16),
            pltpu.VMEM((rows, 128), f32),
        ],
        scratch_shapes=[
            pltpu.VMEM((blocks, feats, 2 * width), bf16),
            pltpu.SemaphoreType.DMA((blocks,)),
            pltpu.SemaphoreType.DMA((blocks,)),
        ],
        compiler_params=PARAMS,
        name="backward",
    )(core, q, got, up, upo, vec, veco, weight, other)


def finish_kernel(back_ref, x_ref, st_ref, gain_ref, target_ref, slot_ref, send_ref):
    blocks = back_ref.shape[0]
    rows, feats = x_ref.shape
    owners = send_ref.shape[0]
    total = back_ref[0].astype(f32)
    for b in range(1, blocks):
        total += back_ref[b].astype(f32)
    tail = total[rows : rows + 8, :rows]
    sums = tail.T / (2 * blocks * feats)
    first = sums[:, 0:1] + sums[:, 1:2]
    second = sums[:, 2:3] + sums[:, 3:4]
    mean, inv_std = st_ref[:, 0:1], st_ref[:, 1:2]
    unit = (x_ref[...].astype(f32) - mean) * inv_std
    grad = (inv_std * (total[:rows] * gain_ref[...] - first - unit * second)).astype(bf16)
    slots = owners * CAPACITY
    placing = lax.broadcasted_iota(jnp.int32, (slots, rows), 0) == target_ref[...]
    placed = jnp.dot(
        jnp.where(placing, 1.0, 0.0).astype(bf16), grad, preferred_element_type=f32
    ).astype(bf16)
    placed = placed.reshape(owners, CAPACITY, feats)
    for k in range(feats // 128):
        send_ref[:, k * CAPACITY : (k + 1) * CAPACITY, :] = placed[:, :, k * 128 : (k + 1) * 128]
    send_ref[:, feats // 128 * CAPACITY :, :] = jnp.broadcast_to(slot_ref[...][:, None, :], (owners, 8, 128))


def finish(back, x, st, gain, target, slot):
    owners = slot.shape[0]
    return pl.pallas_call(
        finish_kernel,
        in_specs=in_vmem(6),
        out_specs=in_vmem(1)[0],
        out_shape=pltpu.VMEM((owners, x.shape[1] // 128 * CAPACITY + 8, 128), bf16),
        compiler_params=PARAMS,
        name="finish",
    )(*held(back, x, st, gain, target, slot))


def landing_kernel(got_ref, o_ref):
    rows, feats = o_ref.shape
    owners = got_ref.shape[0]
    slots = owners * CAPACITY
    pieces = feats // 128
    held_slots = got_ref[:, pieces * CAPACITY, :].astype(bf16)
    spread = lax.broadcasted_iota(jnp.int32, (128, slots), 0) == (
        lax.broadcasted_iota(jnp.int32, (128, slots), 1) % CAPACITY
    )
    every = jnp.dot(held_slots, jnp.where(spread, 1.0, 0.0).astype(bf16), preferred_element_type=f32)
    own = lax.broadcasted_iota(jnp.int32, (owners, slots), 0) == (
        lax.broadcasted_iota(jnp.int32, (owners, slots), 1) // CAPACITY
    )
    slot = jnp.sum(jnp.where(own, every, 0.0), axis=0, keepdims=True).astype(jnp.int32)
    landing = lax.broadcasted_iota(jnp.int32, (rows, slots), 0) == slot
    landing = jnp.where(landing, 1.0, 0.0).astype(bf16)
    for k in range(pieces):
        piece = got_ref[:, k * CAPACITY : (k + 1) * CAPACITY, :].reshape(slots, 128)
        o_ref[:, k * 128 : (k + 1) * 128] = jnp.dot(
            landing, piece, preferred_element_type=f32
        ).astype(bf16)


def land(got, rows, feats):
    return pl.pallas_call(
        landing_kernel,
        in_specs=in_vmem(1),
        out_specs=in_vmem(1)[0],
        out_shape=jax.ShapeDtypeStruct((rows, feats), bf16),
        compiler_params=PARAMS,
        name="land",
    )(*held(got))


def per_device(inputs, upstream, proj_weight, proj_bias, norm_gain, home_rows):
    rows, feats = inputs.shape
    width = upstream.shape[1]
    n_tensor, owners = lax.axis_size("tensor"), lax.axis_size("dp")
    chips = n_tensor // 2
    me = lax.axis_index("tensor")
    core = me % 2
    swap = [(t, t ^ 1) for t in range(n_tensor)]
    classes = [[2 * k + c for k in range(chips)] for c in range(2)]
    core_arr = core.reshape(1).astype(jnp.int32)

    sent = spread(inputs, chips)
    half = lax.all_to_all(sent, "tensor", 0, 0, axis_index_groups=classes, tiled=True)

    pairs = proj_weight.reshape(chips, 2, feats, width)
    cut = lax.dynamic_index_in_dim(pairs, 1 - core, 1, False)
    other = lax.ppermute(cut, "tensor", swap)
    upo = lax.ppermute(upstream, "tensor", swap)
    gains = norm_gain.reshape(chips, 2, 1, feats)
    scales = jnp.sum(norm_gain.reshape(chips, 2, feats, 1) * pairs.astype(f32), axis=(0, 2))
    vec = jnp.concatenate([proj_bias[None], scales], axis=0)
    veco = lax.ppermute(vec, "tensor", swap)

    owner_of = home_rows // rows
    home_slot = home_rows % rows
    order_ids = jnp.arange(rows, dtype=jnp.int32)
    earlier = jnp.sum(
        ((owner_of[:, None] == owner_of[None, :]) & (order_ids[:, None] > order_ids[None, :])).astype(
            jnp.int32
        ),
        axis=1,
    )
    target = owner_of * CAPACITY + earlier
    lanes = jnp.arange(128, dtype=jnp.int32)
    held_at = (jnp.arange(owners, dtype=jnp.int32)[:, None] * CAPACITY + lanes[None, :])[:, :, None]
    match = (held_at == target[None, None, :]) & (lanes < CAPACITY)[None, :, None]
    slot = jnp.sum(jnp.where(match, home_slot[None, None, :] + 1, 0), axis=2) - 1
    slot = slot.astype(f32).astype(bf16)

    own_gain = lax.dynamic_index_in_dim(norm_gain.reshape(n_tensor, 1, feats), me, 0, False)
    half, other, upo, veco, slot, target, own_gain = lax.optimization_barrier(
        (half, other, upo, veco, slot, target, own_gain)
    )
    q = forward(core_arr, half, gains, pairs, other)
    got = lax.ppermute(q, "tensor", swap)
    parts, st = backward(core_arr, q, got, upstream, upo, vec, veco, pairs, other)
    back = lax.all_to_all(parts, "tensor", 0, 0, axis_index_groups=classes, tiled=True)
    send = finish(back, inputs, st, own_gain, target[None, :], slot)
    arrived = lax.all_to_all(send, "dp", split_axis=0, concat_axis=0, tiled=True)
    return land(arrived, rows, feats)


def solution(mesh):
    return jax.shard_map(
        per_device,
        mesh=mesh,
        in_specs=(
            P("dp", "tensor"),
            P("dp", "tensor"),
            P(None, "tensor"),
            P("tensor"),
            P(),
            P("dp"),
        ),
        out_specs=P("dp", "tensor"),
        check_vma=False,
    )
```

```python
import jax
import jax.numpy as jnp
from jax import lax
from jax.experimental import pallas as pl
from jax.experimental.pallas import tpu as pltpu
from jax.sharding import PartitionSpec as P


epsilon = 1e-05
f32, bf16 = jnp.float32, jnp.bfloat16
PAD = 8
CAPACITY = 16
NT = (((1,), (1,)), ((), ()))


def in_vmem(n):
    return [pl.BlockSpec(memory_space=pltpu.VMEM) for _ in range(n)]


def held(*arrays):
    return [pltpu.with_memory_space_constraint(a, pltpu.VMEM) for a in arrays]


PARAMS = pltpu.CompilerParams(vmem_limit_bytes=16 * 1024 * 1024)


ANYWHERE = pl.BlockSpec(memory_space=pl.ANY)
SCALAR = pl.BlockSpec(memory_space=pltpu.SMEM)


def spread_kernel(x_any, o_any, x_ref, in_sem, out_sem):
    blocks, rows, _ = o_any.shape
    parts = in_sem.shape[0]
    step = rows // parts
    loads, stores = [], []
    for p in range(parts):
        span = pl.ds(p * step, step)
        loads.append(pltpu.make_async_copy(x_any.at[span], x_ref.at[span], in_sem.at[p]))
        stores.append(
            [
                pltpu.make_async_copy(x_ref.at[span], o_any.at[b, span], out_sem.at[p, b])
                for b in range(blocks)
            ]
        )
    for copy in loads:
        copy.start()
    for p in range(parts):
        loads[p].wait()
        for copy in stores[p]:
            copy.start()
    for part in stores:
        for copy in part:
            copy.wait()


def spread(x, blocks):
    return pl.pallas_call(
        spread_kernel,
        in_specs=[ANYWHERE],
        out_specs=ANYWHERE,
        out_shape=pltpu.HBM((blocks,) + x.shape, x.dtype),
        scratch_shapes=[
            pltpu.VMEM(x.shape, x.dtype),
            pltpu.SemaphoreType.DMA((2,)),
            pltpu.SemaphoreType.DMA((2, blocks)),
        ],
        compiler_params=PARAMS,
        name="spread",
    )(pltpu.with_memory_space_constraint(x, pltpu.HBM))


def weight_copies(core, weight_any, other_any, weight_ref, w_sem, o_sem):
    blocks, _, width = weight_ref.shape
    half = width // 2
    return [
        (
            pltpu.make_async_copy(weight_any.at[b, core], weight_ref.at[b, :, :half], w_sem.at[b]),
            pltpu.make_async_copy(other_any.at[b], weight_ref.at[b, :, half:], o_sem.at[b]),
        )
        for b in range(blocks)
    ]


def forward_kernel(
    core_ref, x_any, gain_ref, weight_any, other_any, q_ref, x_ref, weight_ref, rows_ref, x_sem, w_sem, o_sem
):
    blocks, rows, feats = x_ref.shape
    width = weight_ref.shape[2]
    half = blocks // 2
    core = core_ref[0]
    x_copies = [pltpu.make_async_copy(x_any.at[b], x_ref.at[b], x_sem.at[b]) for b in range(blocks)]
    w_copies = weight_copies(core, weight_any, other_any, weight_ref, w_sem, o_sem)
    for b in range(blocks):
        x_copies[b].start()
        for copy in w_copies[b]:
            copy.start()
    x_copies[0].wait()
    pivot = jnp.mean(x_ref[0].astype(f32), axis=1, keepdims=True)
    total = jnp.zeros((rows, 128), f32)
    square = jnp.zeros((rows, 128), f32)
    for b in range(blocks):
        if b > 0:
            x_copies[b].wait()
        moved = x_ref[b].astype(f32) - pivot
        for j in range(0, feats, 128):
            part = moved[:, j : j + 128]
            total += part
            square += part * part
        rows_ref[:, b * feats : (b + 1) * feats] = (moved * gain_ref[b, core]).astype(bf16)
        for copy in w_copies[b]:
            copy.wait()
        if b % half == half - 1:
            term = jnp.dot(
                rows_ref[:, (b + 1 - half) * feats : (b + 1) * feats],
                weight_ref[b + 1 - half : b + 1].reshape(half * feats, width),
                preferred_element_type=f32,
            )
            if b < half:
                q_ref[:, :width] = term
            else:
                q_ref[:, :width] += term
    shift = jnp.sum(total, axis=1, keepdims=True) / (blocks * feats)
    spread = jnp.sum(square, axis=1, keepdims=True) / (blocks * feats) - shift * shift
    lane = lax.broadcasted_iota(jnp.int32, (rows, 128), 1)
    q_ref[:, width:] = jnp.where(
        lane == 0, pivot, jnp.where(lane == 1, pivot + shift, jnp.maximum(spread, 0.0))
    )


def forward(core, x, gain, weight, other):
    blocks, rows, feats = x.shape
    width = other.shape[2]
    return pl.pallas_call(
        forward_kernel,
        in_specs=[SCALAR, ANYWHERE] + in_vmem(1) + [ANYWHERE, ANYWHERE],
        out_specs=in_vmem(1)[0],
        out_shape=jax.ShapeDtypeStruct((rows, 2 * width + 128), f32),
        scratch_shapes=[
            pltpu.VMEM(x.shape, bf16),
            pltpu.VMEM((blocks, feats, 2 * width), bf16),
            pltpu.VMEM((rows, blocks * feats), bf16),
            pltpu.SemaphoreType.DMA((blocks,)),
            pltpu.SemaphoreType.DMA((blocks,)),
            pltpu.SemaphoreType.DMA((blocks,)),
        ],
        compiler_params=PARAMS,
        name="forward",
    )(core, x, gain, weight, other)


def backward_kernel(
    core_ref,
    q_ref,
    got_ref,
    up_ref,
    upo_ref,
    vec_ref,
    veco_ref,
    weight_any,
    other_any,
    p_ref,
    st_ref,
    weight_ref,
    w_sem,
    o_sem,
):
    blocks, feats, width = weight_ref.shape
    width = width // 2
    rows = q_ref.shape[0]
    core = core_ref[0]
    w_copies = weight_copies(core, weight_any, other_any, weight_ref, w_sem, o_sem)
    for pair in w_copies:
        for copy in pair:
            copy.start()
    mine, theirs = q_ref[:, 2 * width :], got_ref[:, 2 * width :]
    gap = 0.5 * (mine[:, 1:2] - theirs[:, 1:2])
    mean = 0.5 * (mine[:, 1:2] + theirs[:, 1:2])
    variance = 0.5 * (mine[:, 2:3] + theirs[:, 2:3]) + gap * gap
    inv_std = lax.rsqrt(variance + epsilon)
    lane = lax.broadcasted_iota(jnp.int32, (rows, 128), 1)
    st_ref[...] = jnp.where(lane == 0, mean, inv_std)
    even = jnp.where(core == 0, mine[:, 0:1], theirs[:, 0:1]) - mean
    odd = jnp.where(core == 0, theirs[:, 0:1], mine[:, 0:1]) - mean

    def grad(summed, up, vec):
        raw = inv_std * (summed + even * vec[1:2, :] + odd * vec[2:3, :])
        preact = raw + vec[0:1, :]
        gate = 1.0 / (1.0 + jnp.exp(-preact))
        pg = (up.astype(f32) * gate * (1.0 + preact * (1.0 - gate))).astype(bf16)
        wide = pg.astype(f32)
        scale = vec[1:2, :] + vec[2:3, :]
        return (
            pg,
            jnp.sum(wide * scale, axis=1, keepdims=True),
            jnp.sum(wide * raw, axis=1, keepdims=True),
        )

    pg, sum_g, sum_gu = grad(q_ref[:, :width] + got_ref[:, width : 2 * width], up_ref[...], vec_ref[...])
    pgo, sum_go, sum_guo = grad(
        q_ref[:, width : 2 * width] + got_ref[:, :width], upo_ref[...], veco_ref[...]
    )
    both = jnp.concatenate([pg, pgo], axis=1)
    value = jnp.where(lane < 2, sum_g + sum_go, sum_gu + sum_guo)
    high = value.astype(bf16).astype(f32)
    tail = jnp.where(lane % 2 == 0, high, value - high).T[:PAD].astype(bf16)
    tail = jnp.concatenate([tail, jnp.zeros((PAD, feats - rows), bf16)], axis=1)
    for b in range(blocks):
        for copy in w_copies[b]:
            copy.wait()
        p_ref[b, :rows] = lax.dot_general(both, weight_ref[b], NT, preferred_element_type=f32).astype(bf16)
        p_ref[b, rows:] = tail


def backward(core, q, got, up, upo, vec, veco, weight, other):
    blocks, feats, width = other.shape
    rows = q.shape[0]
    return pl.pallas_call(
        backward_kernel,
        in_specs=[SCALAR] + in_vmem(6) + [ANYWHERE, ANYWHERE],
        out_specs=in_vmem(2),
        out_shape=[
            pltpu.VMEM((blocks, rows + PAD, feats), bf16),
            pltpu.VMEM((rows, 128), f32),
        ],
        scratch_shapes=[
            pltpu.VMEM((blocks, feats, 2 * width), bf16),
            pltpu.SemaphoreType.DMA((blocks,)),
            pltpu.SemaphoreType.DMA((blocks,)),
        ],
        compiler_params=PARAMS,
        name="backward",
    )(core, q, got, up, upo, vec, veco, weight, other)


def finish_kernel(back_ref, x_ref, st_ref, gain_ref, target_ref, slot_ref, send_ref):
    blocks = back_ref.shape[0]
    rows, feats = x_ref.shape
    owners = send_ref.shape[0]
    total = back_ref[0].astype(f32)
    for b in range(1, blocks):
        total += back_ref[b].astype(f32)
    tail = total[rows : rows + 8, :rows]
    sums = tail.T / (2 * blocks * feats)
    first = sums[:, 0:1] + sums[:, 1:2]
    second = sums[:, 2:3] + sums[:, 3:4]
    mean, inv_std = st_ref[:, 0:1], st_ref[:, 1:2]
    unit = (x_ref[...].astype(f32) - mean) * inv_std
    grad = (inv_std * (total[:rows] * gain_ref[...] - first - unit * second)).astype(bf16)
    slots = owners * CAPACITY
    placing = lax.broadcasted_iota(jnp.int32, (slots, rows), 0) == target_ref[...]
    placed = jnp.dot(
        jnp.where(placing, 1.0, 0.0).astype(bf16), grad, preferred_element_type=f32
    ).astype(bf16)
    placed = placed.reshape(owners, CAPACITY, feats)
    for k in range(feats // 128):
        send_ref[:, k * CAPACITY : (k + 1) * CAPACITY, :] = placed[:, :, k * 128 : (k + 1) * 128]
    send_ref[:, feats // 128 * CAPACITY :, :] = jnp.broadcast_to(
        slot_ref[...][:, None, :], (owners, 2, 128)
    )


def finish(back, x, st, gain, target, slot):
    owners = slot.shape[0]
    return pl.pallas_call(
        finish_kernel,
        in_specs=in_vmem(6),
        out_specs=in_vmem(1)[0],
        out_shape=pltpu.VMEM((owners, x.shape[1] // 128 * CAPACITY + 2, 128), bf16),
        compiler_params=PARAMS,
        name="finish",
    )(*held(back, x, st, gain, target, slot))


def landing_kernel(got_ref, o_ref):
    rows, feats = o_ref.shape
    owners = got_ref.shape[0]
    slots = owners * CAPACITY
    pieces = feats // 128
    held_slots = got_ref[:, pieces * CAPACITY, :].astype(bf16)
    spread = lax.broadcasted_iota(jnp.int32, (128, slots), 0) == (
        lax.broadcasted_iota(jnp.int32, (128, slots), 1) % CAPACITY
    )
    every = jnp.dot(held_slots, jnp.where(spread, 1.0, 0.0).astype(bf16), preferred_element_type=f32)
    own = lax.broadcasted_iota(jnp.int32, (owners, slots), 0) == (
        lax.broadcasted_iota(jnp.int32, (owners, slots), 1) // CAPACITY
    )
    slot = jnp.sum(jnp.where(own, every, 0.0), axis=0, keepdims=True).astype(jnp.int32)
    landing = lax.broadcasted_iota(jnp.int32, (rows, slots), 0) == slot
    landing = jnp.where(landing, 1.0, 0.0).astype(bf16)
    for k in range(pieces):
        piece = got_ref[:, k * CAPACITY : (k + 1) * CAPACITY, :].reshape(slots, 128)
        o_ref[:, k * 128 : (k + 1) * 128] = jnp.dot(
            landing, piece, preferred_element_type=f32
        ).astype(bf16)


def land(got, rows, feats):
    return pl.pallas_call(
        landing_kernel,
        in_specs=in_vmem(1),
        out_specs=in_vmem(1)[0],
        out_shape=jax.ShapeDtypeStruct((rows, feats), bf16),
        compiler_params=PARAMS,
        name="land",
    )(*held(got))


def per_device(inputs, upstream, proj_weight, proj_bias, norm_gain, home_rows):
    rows, feats = inputs.shape
    width = upstream.shape[1]
    n_tensor, owners = lax.axis_size("tensor"), lax.axis_size("dp")
    chips = n_tensor // 2
    me = lax.axis_index("tensor")
    core = me % 2
    swap = [(t, t ^ 1) for t in range(n_tensor)]
    classes = [[2 * k + c for k in range(chips)] for c in range(2)]
    core_arr = core.reshape(1).astype(jnp.int32)

    sent = spread(inputs, chips)
    half = lax.all_to_all(sent, "tensor", 0, 0, axis_index_groups=classes, tiled=True)

    pairs = proj_weight.reshape(chips, 2, feats, width)
    cut = lax.dynamic_index_in_dim(pairs, 1 - core, 1, False)
    other = lax.ppermute(cut, "tensor", swap)
    upo = lax.ppermute(upstream, "tensor", swap)
    gains = norm_gain.reshape(chips, 2, 1, feats)
    scales = jnp.sum(norm_gain.reshape(chips, 2, feats, 1) * pairs.astype(f32), axis=(0, 2))
    vec = jnp.concatenate([proj_bias[None], scales], axis=0)
    veco = lax.ppermute(vec, "tensor", swap)

    owner_of = home_rows // rows
    home_slot = home_rows % rows
    order_ids = jnp.arange(rows, dtype=jnp.int32)
    earlier = jnp.sum(
        ((owner_of[:, None] == owner_of[None, :]) & (order_ids[:, None] > order_ids[None, :])).astype(
            jnp.int32
        ),
        axis=1,
    )
    target = owner_of * CAPACITY + earlier
    lanes = jnp.arange(128, dtype=jnp.int32)
    held_at = (jnp.arange(owners, dtype=jnp.int32)[:, None] * CAPACITY + lanes[None, :])[:, :, None]
    match = (held_at == target[None, None, :]) & (lanes < CAPACITY)[None, :, None]
    slot = jnp.sum(jnp.where(match, home_slot[None, None, :] + 1, 0), axis=2) - 1
    slot = slot.astype(f32).astype(bf16)

    own_gain = lax.dynamic_index_in_dim(norm_gain.reshape(n_tensor, 1, feats), me, 0, False)
    half, other, upo, veco, slot, target, own_gain = lax.optimization_barrier(
        (half, other, upo, veco, slot, target, own_gain)
    )
    q = forward(core_arr, half, gains, pairs, other)
    got = lax.ppermute(q, "tensor", swap)
    parts, st = backward(core_arr, q, got, upstream, upo, vec, veco, pairs, other)
    back = lax.all_to_all(parts, "tensor", 0, 0, axis_index_groups=classes, tiled=True)
    send = finish(back, inputs, st, own_gain, target[None, :], slot)
    arrived = lax.all_to_all(send, "dp", split_axis=0, concat_axis=0, tiled=True)
    return land(arrived, rows, feats)


def solution(mesh):
    return jax.shard_map(
        per_device,
        mesh=mesh,
        in_specs=(
            P("dp", "tensor"),
            P("dp", "tensor"),
            P(None, "tensor"),
            P("tensor"),
            P(),
            P("dp"),
        ),
        out_specs=P("dp", "tensor"),
        check_vma=False,
    )
```

```python
import jax
import jax.numpy as jnp
from jax import lax
from jax.experimental import pallas as pl
from jax.experimental.pallas import tpu as pltpu
from jax.sharding import PartitionSpec as P


epsilon = 1e-05
f32, bf16 = jnp.float32, jnp.bfloat16
PAD = 8
CAPACITY = 16
EARLY = 2
NT = (((1,), (1,)), ((), ()))


def in_vmem(n):
    return [pl.BlockSpec(memory_space=pltpu.VMEM) for _ in range(n)]


def held(*arrays):
    return [pltpu.with_memory_space_constraint(a, pltpu.VMEM) for a in arrays]


PARAMS = pltpu.CompilerParams(vmem_limit_bytes=16 * 1024 * 1024)


ANYWHERE = pl.BlockSpec(memory_space=pl.ANY)
SCALAR = pl.BlockSpec(memory_space=pltpu.SMEM)


def spread_kernel(x_any, o_any, x_ref, in_sem, out_sem):
    blocks, rows, _ = o_any.shape
    parts = in_sem.shape[0]
    step = rows // parts
    loads, stores = [], []
    for p in range(parts):
        span = pl.ds(p * step, step)
        loads.append(pltpu.make_async_copy(x_any.at[span], x_ref.at[span], in_sem.at[p]))
        stores.append(
            [
                pltpu.make_async_copy(x_ref.at[span], o_any.at[b, span], out_sem.at[p, b])
                for b in range(blocks)
            ]
        )
    for copy in loads:
        copy.start()
    for p in range(parts):
        loads[p].wait()
        for copy in stores[p]:
            copy.start()
    for part in stores:
        for copy in part:
            copy.wait()


def spread(x, blocks):
    return pl.pallas_call(
        spread_kernel,
        in_specs=[ANYWHERE],
        out_specs=ANYWHERE,
        out_shape=pltpu.HBM((blocks,) + x.shape, x.dtype),
        scratch_shapes=[
            pltpu.VMEM(x.shape, x.dtype),
            pltpu.SemaphoreType.DMA((2,)),
            pltpu.SemaphoreType.DMA((2, blocks)),
        ],
        compiler_params=PARAMS,
        name="spread",
    )(pltpu.with_memory_space_constraint(x, pltpu.HBM))


def weight_copies(core, weight_any, other_any, weight_ref, w_sem, o_sem):
    blocks, _, width = weight_ref.shape
    half = width // 2
    return [
        (
            pltpu.make_async_copy(weight_any.at[b, core], weight_ref.at[b, :, :half], w_sem.at[b]),
            pltpu.make_async_copy(other_any.at[b], weight_ref.at[b, :, half:], o_sem.at[b]),
        )
        for b in range(blocks)
    ]


def forward_kernel(
    core_ref, x_any, gain_ref, weight_any, other_any, q_ref, x_ref, weight_ref, rows_ref, x_sem, w_sem, o_sem
):
    blocks, rows, feats = x_ref.shape
    width = weight_ref.shape[2]
    half = blocks // 2
    core = core_ref[0]
    x_copies = [pltpu.make_async_copy(x_any.at[b], x_ref.at[b], x_sem.at[b]) for b in range(blocks)]
    w_copies = weight_copies(core, weight_any, other_any, weight_ref, w_sem, o_sem)
    for b in range(blocks):
        x_copies[b].start()
        for copy in w_copies[b]:
            copy.start()
    x_copies[0].wait()
    pivot = jnp.mean(x_ref[0].astype(f32), axis=1, keepdims=True)
    total = jnp.zeros((rows, 128), f32)
    square = jnp.zeros((rows, 128), f32)
    for b in range(blocks):
        if b > 0:
            x_copies[b].wait()
        moved = x_ref[b].astype(f32) - pivot
        for j in range(0, feats, 128):
            part = moved[:, j : j + 128]
            total += part
            square += part * part
        rows_ref[:, b * feats : (b + 1) * feats] = (moved * gain_ref[b, core]).astype(bf16)
        for copy in w_copies[b]:
            copy.wait()
        if b % half == half - 1:
            term = jnp.dot(
                rows_ref[:, (b + 1 - half) * feats : (b + 1) * feats],
                weight_ref[b + 1 - half : b + 1].reshape(half * feats, width),
                preferred_element_type=f32,
            )
            if b < half:
                q_ref[:, :width] = term
            else:
                q_ref[:, :width] += term
    shift = jnp.sum(total, axis=1, keepdims=True) / (blocks * feats)
    spread = jnp.sum(square, axis=1, keepdims=True) / (blocks * feats) - shift * shift
    lane = lax.broadcasted_iota(jnp.int32, (rows, 128), 1)
    q_ref[:, width:] = jnp.where(
        lane == 0, pivot, jnp.where(lane == 1, pivot + shift, jnp.maximum(spread, 0.0))
    )


def forward(core, x, gain, weight, other):
    blocks, rows, feats = x.shape
    width = other.shape[2]
    return pl.pallas_call(
        forward_kernel,
        in_specs=[SCALAR, ANYWHERE] + in_vmem(1) + [ANYWHERE, ANYWHERE],
        out_specs=in_vmem(1)[0],
        out_shape=jax.ShapeDtypeStruct((rows, 2 * width + 128), f32),
        scratch_shapes=[
            pltpu.VMEM(x.shape, bf16),
            pltpu.VMEM((blocks, feats, 2 * width), bf16),
            pltpu.VMEM((rows, blocks * feats), bf16),
            pltpu.SemaphoreType.DMA((blocks,)),
            pltpu.SemaphoreType.DMA((blocks,)),
            pltpu.SemaphoreType.DMA((blocks,)),
        ],
        compiler_params=PARAMS,
        name="forward",
    )(core, x, gain, weight, other)


def backward_kernel(
    core_ref,
    q_ref,
    got_ref,
    up_ref,
    upo_ref,
    vec_ref,
    veco_ref,
    weight_any,
    other_any,
    p_any,
    st_ref,
    weight_ref,
    p_ref,
    w_sem,
    o_sem,
    p_sem,
):
    blocks, feats, width = weight_ref.shape
    width = width // 2
    rows = q_ref.shape[0]
    core = core_ref[0]
    w_copies = weight_copies(core, weight_any, other_any, weight_ref, w_sem, o_sem)
    p_copies = [pltpu.make_async_copy(p_ref.at[b], p_any.at[b], p_sem.at[b]) for b in range(blocks)]
    for pair in w_copies:
        for copy in pair:
            copy.start()
    mine, theirs = q_ref[:, 2 * width :], got_ref[:, 2 * width :]
    gap = 0.5 * (mine[:, 1:2] - theirs[:, 1:2])
    mean = 0.5 * (mine[:, 1:2] + theirs[:, 1:2])
    variance = 0.5 * (mine[:, 2:3] + theirs[:, 2:3]) + gap * gap
    inv_std = lax.rsqrt(variance + epsilon)
    lane = lax.broadcasted_iota(jnp.int32, (rows, 128), 1)
    st_ref[...] = jnp.where(lane == 0, mean, inv_std)
    even = jnp.where(core == 0, mine[:, 0:1], theirs[:, 0:1]) - mean
    odd = jnp.where(core == 0, theirs[:, 0:1], mine[:, 0:1]) - mean

    def grad(summed, up, vec):
        raw = inv_std * (summed + even * vec[1:2, :] + odd * vec[2:3, :])
        preact = raw + vec[0:1, :]
        gate = 1.0 / (1.0 + jnp.exp(-preact))
        pg = (up.astype(f32) * gate * (1.0 + preact * (1.0 - gate))).astype(bf16)
        wide = pg.astype(f32)
        scale = vec[1:2, :] + vec[2:3, :]
        return (
            pg,
            jnp.sum(wide * scale, axis=1, keepdims=True),
            jnp.sum(wide * raw, axis=1, keepdims=True),
        )

    pg, sum_g, sum_gu = grad(q_ref[:, :width] + got_ref[:, width : 2 * width], up_ref[...], vec_ref[...])
    pgo, sum_go, sum_guo = grad(
        q_ref[:, width : 2 * width] + got_ref[:, :width], upo_ref[...], veco_ref[...]
    )
    both = jnp.concatenate([pg, pgo], axis=1)
    value = jnp.where(lane < 2, sum_g + sum_go, sum_gu + sum_guo)
    high = value.astype(bf16).astype(f32)
    tail = jnp.where(lane % 2 == 0, high, value - high).T[:PAD].astype(bf16)
    tail = jnp.concatenate([tail, jnp.zeros((PAD, feats - rows), bf16)], axis=1)
    for b in range(blocks):
        for copy in w_copies[b]:
            copy.wait()
        p_ref[b, :rows] = lax.dot_general(both, weight_ref[b], NT, preferred_element_type=f32).astype(bf16)
        p_ref[b, rows:] = tail
        p_copies[b].start()
    for copy in p_copies:
        copy.wait()


def backward(core, q, got, up, upo, vec, veco, weight, other):
    blocks, feats, width = other.shape
    rows = q.shape[0]
    return pl.pallas_call(
        backward_kernel,
        in_specs=[SCALAR] + in_vmem(6) + [ANYWHERE, ANYWHERE],
        out_specs=[ANYWHERE] + in_vmem(1),
        out_shape=[
            pltpu.HBM((blocks, rows + PAD, feats), bf16),
            pltpu.VMEM((rows, 128), f32),
        ],
        scratch_shapes=[
            pltpu.VMEM((blocks, feats, 2 * width), bf16),
            pltpu.VMEM((blocks, rows + PAD, feats), bf16),
            pltpu.SemaphoreType.DMA((blocks,)),
            pltpu.SemaphoreType.DMA((blocks,)),
            pltpu.SemaphoreType.DMA((blocks,)),
        ],
        compiler_params=PARAMS,
        name="backward",
    )(core, q, got, up, upo, vec, veco, weight, other)


def finish_kernel(back_ref, x_any, st_ref, gain_ref, target_ref, send_ref, x_ref, sem):
    fetch = pltpu.make_async_copy(x_any, x_ref, sem)
    fetch.start()
    blocks = back_ref.shape[0]
    rows, feats = x_ref.shape
    owners = send_ref.shape[0]
    total = back_ref[0].astype(f32)
    for b in range(1, blocks):
        total += back_ref[b].astype(f32)
    tail = total[rows : rows + 8, :rows]
    sums = tail.T / (2 * blocks * feats)
    first = sums[:, 0:1] + sums[:, 1:2]
    second = sums[:, 2:3] + sums[:, 3:4]
    mean, inv_std = st_ref[:, 0:1], st_ref[:, 1:2]
    fetch.wait()
    unit = (x_ref[...].astype(f32) - mean) * inv_std
    grad = (inv_std * (total[:rows] * gain_ref[...] - first - unit * second)).astype(bf16)
    slots = owners * CAPACITY
    placing = lax.broadcasted_iota(jnp.int32, (slots, rows), 0) == target_ref[...]
    placed = jnp.dot(
        jnp.where(placing, 1.0, 0.0).astype(bf16), grad, preferred_element_type=f32
    ).astype(bf16)
    placed = placed.reshape(owners, CAPACITY, feats)
    for k in range(feats // 128):
        send_ref[:, k * CAPACITY : (k + 1) * CAPACITY, :] = placed[:, :, k * 128 : (k + 1) * 128]


def finish(back, x, st, gain, target, owners):
    return pl.pallas_call(
        finish_kernel,
        in_specs=in_vmem(1) + [ANYWHERE] + in_vmem(3),
        out_specs=in_vmem(1)[0],
        scratch_shapes=[pltpu.VMEM(x.shape, x.dtype), pltpu.SemaphoreType.DMA],
        out_shape=pltpu.VMEM((owners, x.shape[1] // 128 * CAPACITY, 128), bf16),
        compiler_params=PARAMS,
        name="finish",
    )(*held(back), pltpu.with_memory_space_constraint(x, pltpu.HBM), *held(st, gain, target))


def landing_kernel(got_ref, slot_ref, o_ref):
    rows, feats = o_ref.shape
    slots = slot_ref.shape[1]
    landing = lax.broadcasted_iota(jnp.int32, (rows, slots), 0) == slot_ref[...]
    landing = jnp.where(landing, 1.0, 0.0).astype(bf16)
    for k in range(feats // 128):
        piece = got_ref[:, k * CAPACITY : (k + 1) * CAPACITY, :].reshape(slots, 128)
        o_ref[:, k * 128 : (k + 1) * 128] = jnp.dot(
            landing, piece, preferred_element_type=f32
        ).astype(bf16)


def land(got, slot, rows, feats):
    return pl.pallas_call(
        landing_kernel,
        in_specs=in_vmem(2),
        out_specs=in_vmem(1)[0],
        out_shape=jax.ShapeDtypeStruct((rows, feats), bf16),
        compiler_params=PARAMS,
        name="land",
    )(*held(got, slot))


def arriving_slots(listed, rows):
    owners = listed.shape[0]
    me = lax.axis_index("dp")
    ids = jnp.arange(rows, dtype=jnp.int32)
    mine = listed // rows == me
    below = (ids[:, None] < ids[None, :]).astype(bf16)
    rank = jnp.dot(mine.astype(bf16), below, preferred_element_type=f32).astype(jnp.int32)
    places = jnp.arange(CAPACITY, dtype=jnp.int32)[None, :, None]
    match = mine[:, None, :] & (rank[:, None, :] == places)
    slot = jnp.sum(jnp.where(match, listed[:, None, :] % rows + 1, 0), axis=2) - 1
    index = jnp.arange(owners, dtype=jnp.int32)
    source = (me - index[:, None]) % owners == index[None, :]
    return jnp.sum(jnp.where(source[:, :, None], slot[None], 0), axis=1).reshape(1, -1)


def per_device(inputs, upstream, proj_weight, proj_bias, norm_gain, home_rows):
    rows, feats = inputs.shape
    width = upstream.shape[1]
    n_tensor, owners = lax.axis_size("tensor"), lax.axis_size("dp")
    chips = n_tensor // 2
    me = lax.axis_index("tensor")
    core = me % 2
    swap = [(t, t ^ 1) for t in range(n_tensor)]
    classes = [[2 * k + c for k in range(chips)] for c in range(2)]
    core_arr = core.reshape(1).astype(jnp.int32)

    sent = spread(inputs, chips)
    half = lax.all_to_all(sent, "tensor", 0, 0, axis_index_groups=classes, tiled=True)

    pairs = proj_weight.reshape(chips, 2, feats, width)
    cut = lax.dynamic_index_in_dim(pairs, 1 - core, 1, False)
    other = lax.ppermute(cut, "tensor", swap)
    upo = lax.ppermute(upstream, "tensor", swap)
    gains = norm_gain.reshape(chips, 2, 1, feats)
    scales = jnp.sum(norm_gain.reshape(chips, 2, feats, 1) * pairs.astype(f32), axis=(0, 2))
    vec = jnp.concatenate([proj_bias[None], scales], axis=0)
    veco = lax.ppermute(vec, "tensor", swap)

    owner_of = home_rows // rows
    order_ids = jnp.arange(rows, dtype=jnp.int32)
    earlier = jnp.sum(
        ((owner_of[:, None] == owner_of[None, :]) & (order_ids[:, None] > order_ids[None, :])).astype(
            jnp.int32
        ),
        axis=1,
    )
    target = owner_of * CAPACITY + earlier

    def doubled(listed, step):
        hop = [(d, (d + 2**step) % owners) for d in range(owners)]
        return jnp.concatenate([listed, lax.ppermute(listed, "dp", hop)], axis=0)

    steps = owners.bit_length() - 1
    listed = home_rows[None]
    for step in range(EARLY):
        listed = doubled(listed, step)

    own_gain = lax.dynamic_index_in_dim(norm_gain.reshape(n_tensor, 1, feats), me, 0, False)
    half, other, upo, veco, listed, target, own_gain = lax.optimization_barrier(
        (half, other, upo, veco, listed, target, own_gain)
    )
    q = forward(core_arr, half, gains, pairs, other)
    got = lax.ppermute(q, "tensor", swap)
    parts, st = backward(core_arr, q, got, upstream, upo, vec, veco, pairs, other)
    parts, listed = lax.optimization_barrier((parts, listed))
    back = lax.all_to_all(parts, "tensor", 0, 0, axis_index_groups=classes, tiled=True)
    for step in range(EARLY, steps):
        listed = doubled(listed, step)
    slot = arriving_slots(listed, rows)
    back, slot = lax.optimization_barrier((back, slot))
    send = finish(back, inputs, st, own_gain, target[None, :], owners)
    arrived = lax.all_to_all(send, "dp", split_axis=0, concat_axis=0, tiled=True)
    return land(arrived, slot, rows, feats)


def solution(mesh):
    return jax.shard_map(
        per_device,
        mesh=mesh,
        in_specs=(
            P("dp", "tensor"),
            P("dp", "tensor"),
            P(None, "tensor"),
            P("tensor"),
            P(),
            P("dp"),
        ),
        out_specs=P("dp", "tensor"),
        check_vma=False,
    )
```

```python
import jax
import jax.numpy as jnp
from jax import lax
from jax.experimental import pallas as pl
from jax.experimental.pallas import tpu as pltpu
from jax.sharding import PartitionSpec as P


epsilon = 1e-05
f32, bf16 = jnp.float32, jnp.bfloat16
PAD = 8
CAPACITY = 16
EARLY = 3
NT = (((1,), (1,)), ((), ()))


def in_vmem(n):
    return [pl.BlockSpec(memory_space=pltpu.VMEM) for _ in range(n)]


def held(*arrays):
    return [pltpu.with_memory_space_constraint(a, pltpu.VMEM) for a in arrays]


def far(*arrays):
    return [pltpu.with_memory_space_constraint(a, pltpu.HBM) for a in arrays]


PARAMS = pltpu.CompilerParams(vmem_limit_bytes=16 * 1024 * 1024)


ANYWHERE = pl.BlockSpec(memory_space=pl.ANY)
SCALAR = pl.BlockSpec(memory_space=pltpu.SMEM)


def spread_kernel(x_any, o_any, x_ref, in_sem, out_sem):
    blocks, rows, _ = o_any.shape
    parts = in_sem.shape[0]
    step = rows // parts
    loads, stores = [], []
    for p in range(parts):
        span = pl.ds(p * step, step)
        loads.append(pltpu.make_async_copy(x_any.at[span], x_ref.at[span], in_sem.at[p]))
        stores.append(
            [
                pltpu.make_async_copy(x_ref.at[span], o_any.at[b, span], out_sem.at[p, b])
                for b in range(blocks)
            ]
        )
    for copy in loads:
        copy.start()
    for p in range(parts):
        loads[p].wait()
        for copy in stores[p]:
            copy.start()
    for part in stores:
        for copy in part:
            copy.wait()


def spread(x, blocks):
    return pl.pallas_call(
        spread_kernel,
        in_specs=[ANYWHERE],
        out_specs=ANYWHERE,
        out_shape=pltpu.HBM((blocks,) + x.shape, x.dtype),
        scratch_shapes=[
            pltpu.VMEM(x.shape, x.dtype),
            pltpu.SemaphoreType.DMA((2,)),
            pltpu.SemaphoreType.DMA((2, blocks)),
        ],
        compiler_params=PARAMS,
        name="spread",
    )(pltpu.with_memory_space_constraint(x, pltpu.HBM))


def weight_copies(core, weight_any, other_any, weight_ref, w_sem, o_sem):
    blocks, _, width = weight_ref.shape
    half = width // 2
    return [
        (
            pltpu.make_async_copy(weight_any.at[b, core], weight_ref.at[b, :, :half], w_sem.at[b]),
            pltpu.make_async_copy(other_any.at[b], weight_ref.at[b, :, half:], o_sem.at[b]),
        )
        for b in range(blocks)
    ]


def forward_kernel(
    core_ref, x_any, gain_ref, weight_any, other_any, q_ref, x_ref, weight_ref, rows_ref, x_sem, w_sem, o_sem
):
    blocks, rows, feats = x_ref.shape
    width = weight_ref.shape[2]
    half = blocks // 2
    core = core_ref[0]
    x_copies = [pltpu.make_async_copy(x_any.at[b], x_ref.at[b], x_sem.at[b]) for b in range(blocks)]
    w_copies = weight_copies(core, weight_any, other_any, weight_ref, w_sem, o_sem)
    for b in range(blocks):
        x_copies[b].start()
        for copy in w_copies[b]:
            copy.start()
    x_copies[0].wait()
    pivot = jnp.mean(x_ref[0].astype(f32), axis=1, keepdims=True)
    total = jnp.zeros((rows, 128), f32)
    square = jnp.zeros((rows, 128), f32)
    for b in range(blocks):
        if b > 0:
            x_copies[b].wait()
        moved = x_ref[b].astype(f32) - pivot
        for j in range(0, feats, 128):
            part = moved[:, j : j + 128]
            total += part
            square += part * part
        rows_ref[:, b * feats : (b + 1) * feats] = (moved * gain_ref[b, core]).astype(bf16)
        for copy in w_copies[b]:
            copy.wait()
        if b % half == half - 1:
            term = jnp.dot(
                rows_ref[:, (b + 1 - half) * feats : (b + 1) * feats],
                weight_ref[b + 1 - half : b + 1].reshape(half * feats, width),
                preferred_element_type=f32,
            )
            if b < half:
                q_ref[:, :width] = term
            else:
                q_ref[:, :width] += term
    shift = jnp.sum(total, axis=1, keepdims=True) / (blocks * feats)
    spread = jnp.sum(square, axis=1, keepdims=True) / (blocks * feats) - shift * shift
    lane = lax.broadcasted_iota(jnp.int32, (rows, 128), 1)
    q_ref[:, width:] = jnp.where(
        lane == 0, pivot, jnp.where(lane == 1, pivot + shift, jnp.maximum(spread, 0.0))
    )


def forward(core, x, gain, weight, other):
    blocks, rows, feats = x.shape
    width = other.shape[2]
    return pl.pallas_call(
        forward_kernel,
        in_specs=[SCALAR, ANYWHERE] + in_vmem(1) + [ANYWHERE, ANYWHERE],
        out_specs=in_vmem(1)[0],
        out_shape=pltpu.VMEM((rows, 2 * width + 128), f32),
        scratch_shapes=[
            pltpu.VMEM(x.shape, bf16),
            pltpu.VMEM((blocks, feats, 2 * width), bf16),
            pltpu.VMEM((rows, blocks * feats), bf16),
            pltpu.SemaphoreType.DMA((blocks,)),
            pltpu.SemaphoreType.DMA((blocks,)),
            pltpu.SemaphoreType.DMA((blocks,)),
        ],
        compiler_params=PARAMS,
        name="forward",
    )(core, x, gain, *far(weight), other)


def backward_kernel(
    core_ref,
    q_ref,
    got_ref,
    up_ref,
    upo_ref,
    vec_ref,
    veco_ref,
    weight_any,
    other_any,
    p_any,
    st_ref,
    weight_ref,
    p_ref,
    w_sem,
    o_sem,
    p_sem,
):
    blocks, feats, width = weight_ref.shape
    width = width // 2
    rows = q_ref.shape[0]
    core = core_ref[0]
    w_copies = weight_copies(core, weight_any, other_any, weight_ref, w_sem, o_sem)
    p_copies = [pltpu.make_async_copy(p_ref.at[b], p_any.at[b], p_sem.at[b]) for b in range(blocks)]
    for pair in w_copies:
        for copy in pair:
            copy.start()
    mine, theirs = q_ref[:, 2 * width :], got_ref[:, 2 * width :]
    gap = 0.5 * (mine[:, 1:2] - theirs[:, 1:2])
    mean = 0.5 * (mine[:, 1:2] + theirs[:, 1:2])
    variance = 0.5 * (mine[:, 2:3] + theirs[:, 2:3]) + gap * gap
    inv_std = lax.rsqrt(variance + epsilon)
    lane = lax.broadcasted_iota(jnp.int32, (rows, 128), 1)
    st_ref[...] = jnp.where(lane == 0, mean, inv_std)
    even = jnp.where(core == 0, mine[:, 0:1], theirs[:, 0:1]) - mean
    odd = jnp.where(core == 0, theirs[:, 0:1], mine[:, 0:1]) - mean

    def grad(summed, up, vec):
        raw = inv_std * (summed + even * vec[1:2, :] + odd * vec[2:3, :])
        preact = raw + vec[0:1, :]
        gate = 1.0 / (1.0 + jnp.exp(-preact))
        pg = (up.astype(f32) * gate * (1.0 + preact * (1.0 - gate))).astype(bf16)
        wide = pg.astype(f32)
        scale = vec[1:2, :] + vec[2:3, :]
        return (
            pg,
            jnp.sum(wide * scale, axis=1, keepdims=True),
            jnp.sum(wide * raw, axis=1, keepdims=True),
        )

    pg, sum_g, sum_gu = grad(q_ref[:, :width] + got_ref[:, width : 2 * width], up_ref[...], vec_ref[...])
    pgo, sum_go, sum_guo = grad(
        q_ref[:, width : 2 * width] + got_ref[:, :width], upo_ref[...], veco_ref[...]
    )
    both = jnp.concatenate([pg, pgo], axis=1)
    value = jnp.where(lane < 2, sum_g + sum_go, sum_gu + sum_guo)
    high = value.astype(bf16).astype(f32)
    tail = jnp.where(lane % 2 == 0, high, value - high).T[:PAD].astype(bf16)
    tail = jnp.concatenate([tail, jnp.zeros((PAD, feats - rows), bf16)], axis=1)
    for b in range(blocks):
        for copy in w_copies[b]:
            copy.wait()
        p_ref[b, :rows] = lax.dot_general(both, weight_ref[b], NT, preferred_element_type=f32).astype(bf16)
        p_ref[b, rows:] = tail
        p_copies[b].start()
    for copy in p_copies:
        copy.wait()


def backward(core, q, got, up, upo, vec, veco, weight, other):
    blocks, feats, width = other.shape
    rows = q.shape[0]
    return pl.pallas_call(
        backward_kernel,
        in_specs=[SCALAR] + in_vmem(6) + [ANYWHERE, ANYWHERE],
        out_specs=[ANYWHERE] + in_vmem(1),
        out_shape=[
            pltpu.HBM((blocks, rows + PAD, feats), bf16),
            pltpu.VMEM((rows, 128), f32),
        ],
        scratch_shapes=[
            pltpu.VMEM((blocks, feats, 2 * width), bf16),
            pltpu.VMEM((blocks, rows + PAD, feats), bf16),
            pltpu.SemaphoreType.DMA((blocks,)),
            pltpu.SemaphoreType.DMA((blocks,)),
            pltpu.SemaphoreType.DMA((blocks,)),
        ],
        compiler_params=PARAMS,
        name="backward",
    )(core, q, got, up, upo, vec, veco, *far(weight), other)


def finish_kernel(back_ref, x_ref, st_ref, gain_ref, target_ref, send_ref):
    blocks = back_ref.shape[0]
    rows, feats = x_ref.shape
    owners = send_ref.shape[0]
    total = back_ref[0].astype(f32)
    for b in range(1, blocks):
        total += back_ref[b].astype(f32)
    tail = total[rows : rows + 8, :rows]
    sums = tail.T / (2 * blocks * feats)
    first = sums[:, 0:1] + sums[:, 1:2]
    second = sums[:, 2:3] + sums[:, 3:4]
    mean, inv_std = st_ref[:, 0:1], st_ref[:, 1:2]
    unit = (x_ref[...].astype(f32) - mean) * inv_std
    grad = (inv_std * (total[:rows] * gain_ref[...] - first - unit * second)).astype(bf16)
    slots = owners * CAPACITY
    placing = lax.broadcasted_iota(jnp.int32, (slots, rows), 0) == target_ref[...]
    placed = jnp.dot(
        jnp.where(placing, 1.0, 0.0).astype(bf16), grad, preferred_element_type=f32
    ).astype(bf16)
    placed = placed.reshape(owners, CAPACITY, feats)
    for k in range(feats // 128):
        send_ref[:, k * CAPACITY : (k + 1) * CAPACITY, :] = placed[:, :, k * 128 : (k + 1) * 128]


def finish(back, x, st, gain, target, owners):
    return pl.pallas_call(
        finish_kernel,
        in_specs=in_vmem(5),
        out_specs=in_vmem(1)[0],
        out_shape=pltpu.VMEM((owners, x.shape[1] // 128 * CAPACITY, 128), bf16),
        compiler_params=PARAMS,
        name="finish",
    )(*held(back, x, st, gain, target))


def landing_kernel(got_ref, slot_ref, o_ref):
    rows, feats = o_ref.shape
    slots = slot_ref.shape[1]
    landing = lax.broadcasted_iota(jnp.int32, (rows, slots), 0) == slot_ref[...]
    landing = jnp.where(landing, 1.0, 0.0).astype(bf16)
    for k in range(feats // 128):
        piece = got_ref[:, k * CAPACITY : (k + 1) * CAPACITY, :].reshape(slots, 128)
        o_ref[:, k * 128 : (k + 1) * 128] = jnp.dot(
            landing, piece, preferred_element_type=f32
        ).astype(bf16)


def land(got, slot, rows, feats):
    return pl.pallas_call(
        landing_kernel,
        in_specs=in_vmem(2),
        out_specs=in_vmem(1)[0],
        out_shape=jax.ShapeDtypeStruct((rows, feats), bf16),
        compiler_params=PARAMS,
        name="land",
    )(*held(got, slot))


def arriving_slots(listed, rows):
    owners = listed.shape[0]
    me = lax.axis_index("dp")
    ids = jnp.arange(rows, dtype=jnp.int32)
    mine = listed // rows == me
    below = (ids[:, None] < ids[None, :]).astype(bf16)
    rank = jnp.dot(mine.astype(bf16), below, preferred_element_type=f32).astype(jnp.int32)
    places = jnp.arange(CAPACITY, dtype=jnp.int32)[None, :, None]
    match = mine[:, None, :] & (rank[:, None, :] == places)
    slot = jnp.sum(jnp.where(match, listed[:, None, :] % rows + 1, 0), axis=2) - 1
    index = jnp.arange(owners, dtype=jnp.int32)
    source = (me - index[:, None]) % owners == index[None, :]
    return jnp.sum(jnp.where(source[:, :, None], slot[None], 0), axis=1).reshape(1, -1)


def per_device(inputs, upstream, proj_weight, proj_bias, norm_gain, home_rows):
    rows, feats = inputs.shape
    width = upstream.shape[1]
    n_tensor, owners = lax.axis_size("tensor"), lax.axis_size("dp")
    chips = n_tensor // 2
    me = lax.axis_index("tensor")
    core = me % 2
    swap = [(t, t ^ 1) for t in range(n_tensor)]
    classes = [[2 * k + c for k in range(chips)] for c in range(2)]
    core_arr = core.reshape(1).astype(jnp.int32)

    sent = spread(inputs, chips)
    half = lax.all_to_all(sent, "tensor", 0, 0, axis_index_groups=classes, tiled=True)

    pairs = proj_weight.reshape(chips, 2, feats, width)
    cut = lax.dynamic_index_in_dim(pairs, 1 - core, 1, False)
    other = lax.ppermute(cut, "tensor", swap)
    upo = lax.ppermute(upstream, "tensor", swap)
    gains = norm_gain.reshape(chips, 2, 1, feats)
    scales = jnp.sum(norm_gain.reshape(chips, 2, feats, 1) * pairs.astype(f32), axis=(0, 2))
    vec = jnp.concatenate([proj_bias[None], scales], axis=0)
    veco = lax.ppermute(vec, "tensor", swap)

    owner_of = home_rows // rows
    order_ids = jnp.arange(rows, dtype=jnp.int32)
    earlier = jnp.sum(
        ((owner_of[:, None] == owner_of[None, :]) & (order_ids[:, None] > order_ids[None, :])).astype(
            jnp.int32
        ),
        axis=1,
    )
    target = owner_of * CAPACITY + earlier

    def doubled(listed, step):
        hop = [(d, (d + 2**step) % owners) for d in range(owners)]
        return jnp.concatenate([listed, lax.ppermute(listed, "dp", hop)], axis=0)

    steps = owners.bit_length() - 1
    listed = home_rows[None]
    for step in range(EARLY):
        listed = doubled(listed, step)

    own_gain = lax.dynamic_index_in_dim(norm_gain.reshape(n_tensor, 1, feats), me, 0, False)
    half, other, upo, veco, listed, target, own_gain = lax.optimization_barrier(
        (half, other, upo, veco, listed, target, own_gain)
    )
    q = forward(core_arr, half, gains, pairs, other)
    got = lax.ppermute(q, "tensor", swap)
    parts, st = backward(core_arr, q, got, upstream, upo, vec, veco, pairs, other)
    parts, listed = lax.optimization_barrier((parts, listed))
    back = lax.all_to_all(parts, "tensor", 0, 0, axis_index_groups=classes, tiled=True)
    for step in range(EARLY, steps):
        listed = doubled(listed, step)
    slot = arriving_slots(listed, rows)
    back, slot = lax.optimization_barrier((back, slot))
    send = finish(back, inputs, st, own_gain, target[None, :], owners)
    arrived = lax.all_to_all(send, "dp", split_axis=0, concat_axis=0, tiled=True)
    return land(arrived, slot, rows, feats)


def solution(mesh):
    return jax.shard_map(
        per_device,
        mesh=mesh,
        in_specs=(
            P("dp", "tensor"),
            P("dp", "tensor"),
            P(None, "tensor"),
            P("tensor"),
            P(),
            P("dp"),
        ),
        out_specs=P("dp", "tensor"),
        check_vma=False,
    )
```

```python
import jax
import jax.numpy as jnp
from jax import lax
from jax.experimental import pallas as pl
from jax.experimental.pallas import tpu as pltpu
from jax.sharding import PartitionSpec as P


epsilon = 1e-05
f32, bf16 = jnp.float32, jnp.bfloat16
PAD = 8
CAPACITY = 16
NT = (((1,), (1,)), ((), ()))


def in_vmem(n):
    return [pl.BlockSpec(memory_space=pltpu.VMEM) for _ in range(n)]


def held(*arrays):
    return [pltpu.with_memory_space_constraint(a, pltpu.VMEM) for a in arrays]


def far(*arrays):
    return [pltpu.with_memory_space_constraint(a, pltpu.HBM) for a in arrays]


PARAMS = pltpu.CompilerParams(vmem_limit_bytes=16 * 1024 * 1024)


ANYWHERE = pl.BlockSpec(memory_space=pl.ANY)
SCALAR = pl.BlockSpec(memory_space=pltpu.SMEM)


def spread_kernel(x_any, o_any, x_ref, in_sem, out_sem):
    blocks, rows, _ = o_any.shape
    parts = in_sem.shape[0]
    step = rows // parts
    loads, stores = [], []
    for p in range(parts):
        span = pl.ds(p * step, step)
        loads.append(pltpu.make_async_copy(x_any.at[span], x_ref.at[span], in_sem.at[p]))
        stores.append(
            [
                pltpu.make_async_copy(x_ref.at[span], o_any.at[b, span], out_sem.at[p, b])
                for b in range(blocks)
            ]
        )
    for copy in loads:
        copy.start()
    for p in range(parts):
        loads[p].wait()
        for copy in stores[p]:
            copy.start()
    for part in stores:
        for copy in part:
            copy.wait()


def spread(x, blocks):
    return pl.pallas_call(
        spread_kernel,
        in_specs=[ANYWHERE],
        out_specs=ANYWHERE,
        out_shape=pltpu.HBM((blocks,) + x.shape, x.dtype),
        scratch_shapes=[
            pltpu.VMEM(x.shape, x.dtype),
            pltpu.SemaphoreType.DMA((2,)),
            pltpu.SemaphoreType.DMA((2, blocks)),
        ],
        compiler_params=PARAMS,
        name="spread",
    )(pltpu.with_memory_space_constraint(x, pltpu.HBM))


def prepare_kernel(core_ref, w_any, gain_ref, bias_ref, cut_any, vec_ref, w_ref, w_sem, cut_sem):
    blocks, _, feats, width = w_ref.shape
    core = core_ref[0]
    loads = [pltpu.make_async_copy(w_any.at[b], w_ref.at[b], w_sem.at[b]) for b in range(blocks)]
    stores = [
        pltpu.make_async_copy(w_ref.at[b, 1 - core], cut_any.at[b], cut_sem.at[b]) for b in range(blocks)
    ]
    for copy in loads:
        copy.start()
    row = lax.broadcasted_iota(jnp.int32, (8, feats), 0)
    totals = [jnp.zeros((8, width), f32), jnp.zeros((8, width), f32)]
    for b in range(blocks):
        loads[b].wait()
        stores[b].start()
        for c in range(2):
            gain = jnp.broadcast_to(gain_ref[b, c], (8, feats))
            high = gain.astype(bf16).astype(f32)
            middle = (gain - high).astype(bf16).astype(f32)
            low = gain - high - middle
            pieces = jnp.where(row == 0, high, jnp.where(row == 1, middle, jnp.where(row == 2, low, 0.0)))
            totals[c] += jnp.dot(pieces.astype(bf16), w_ref[b, c], preferred_element_type=f32)
    line = lax.broadcasted_iota(jnp.int32, (8, width), 0)
    even = jnp.sum(totals[0], axis=0, keepdims=True)
    odd = jnp.sum(totals[1], axis=0, keepdims=True)
    vec_ref[...] = jnp.where(line == 0, bias_ref[...], jnp.where(line == 1, even, odd))
    for copy in stores:
        copy.wait()


def prepare(core, weight, gain, bias):
    blocks, _, feats, width = weight.shape
    return pl.pallas_call(
        prepare_kernel,
        in_specs=[SCALAR, ANYWHERE] + in_vmem(2),
        out_specs=[ANYWHERE] + in_vmem(1),
        out_shape=[
            pltpu.HBM((blocks, feats, width), weight.dtype),
            jax.ShapeDtypeStruct((8, width), f32),
        ],
        scratch_shapes=[
            pltpu.VMEM(weight.shape, weight.dtype),
            pltpu.SemaphoreType.DMA((blocks,)),
            pltpu.SemaphoreType.DMA((blocks,)),
        ],
        compiler_params=PARAMS,
        name="prepare",
    )(core, *far(weight), gain, bias)


def weight_copies(core, weight_any, weight_ref, w_sem):
    blocks = weight_ref.shape[0]
    return [
        pltpu.make_async_copy(weight_any.at[b, core], weight_ref.at[b], w_sem.at[b]) for b in range(blocks)
    ]


def forward_kernel(core_ref, x_ref, gain_ref, weight_any, other_ref, q_ref, weight_ref, rows_ref, w_sem):
    blocks, rows, feats = x_ref.shape
    width = weight_ref.shape[2]
    core = core_ref[0]
    w_copies = weight_copies(core, weight_any, weight_ref, w_sem)
    for copy in w_copies:
        copy.start()
    pivot = jnp.mean(x_ref[0].astype(f32), axis=1, keepdims=True)
    total = jnp.zeros((rows, 128), f32)
    square = jnp.zeros((rows, 128), f32)
    for b in range(blocks):
        moved = x_ref[b].astype(f32) - pivot
        for j in range(0, feats, 128):
            part = moved[:, j : j + 128]
            total += part
            square += part * part
        rows_ref[:, b * feats : (b + 1) * feats] = (moved * gain_ref[b, core]).astype(bf16)
        if b % 2 == 1:
            term = jnp.dot(
                rows_ref[:, (b - 1) * feats : (b + 1) * feats],
                other_ref[b - 1 : b + 1].reshape(2 * feats, width),
                preferred_element_type=f32,
            )
            if b == 1:
                q_ref[:, width : 2 * width] = term
            else:
                q_ref[:, width : 2 * width] += term
    shift = jnp.sum(total, axis=1, keepdims=True) / (blocks * feats)
    spread = jnp.sum(square, axis=1, keepdims=True) / (blocks * feats) - shift * shift
    lane = lax.broadcasted_iota(jnp.int32, (rows, 128), 1)
    q_ref[:, 2 * width :] = jnp.where(
        lane == 0, pivot, jnp.where(lane == 1, pivot + shift, jnp.maximum(spread, 0.0))
    )
    for copy in w_copies:
        copy.wait()
    q_ref[:, :width] = jnp.dot(
        rows_ref[...], weight_ref[...].reshape(blocks * feats, width), preferred_element_type=f32
    )


def forward(core, x, gain, weight, other):
    blocks, rows, feats = x.shape
    width = other.shape[2]
    x, other = held(x, other)
    return pl.pallas_call(
        forward_kernel,
        in_specs=[SCALAR] + in_vmem(2) + [ANYWHERE] + in_vmem(1),
        out_specs=in_vmem(1)[0],
        out_shape=jax.ShapeDtypeStruct((rows, 2 * width + 128), f32),
        scratch_shapes=[
            pltpu.VMEM(other.shape, bf16),
            pltpu.VMEM((rows, blocks * feats), bf16),
            pltpu.SemaphoreType.DMA((blocks,)),
        ],
        compiler_params=PARAMS,
        name="forward",
    )(core, x, gain, *far(weight), other)


def backward_kernel(
    core_ref,
    q_ref,
    got_ref,
    up_ref,
    upo_ref,
    vec_ref,
    veco_ref,
    weight_any,
    other_ref,
    p_ref,
    st_ref,
    weight_ref,
    w_sem,
):
    blocks, feats, width = weight_ref.shape
    rows = q_ref.shape[0]
    core = core_ref[0]
    w_copies = weight_copies(core, weight_any, weight_ref, w_sem)
    for copy in w_copies:
        copy.start()
    mine, theirs = q_ref[:, 2 * width :], got_ref[:, 2 * width :]
    gap = 0.5 * (mine[:, 1:2] - theirs[:, 1:2])
    mean = 0.5 * (mine[:, 1:2] + theirs[:, 1:2])
    variance = 0.5 * (mine[:, 2:3] + theirs[:, 2:3]) + gap * gap
    inv_std = lax.rsqrt(variance + epsilon)
    lane = lax.broadcasted_iota(jnp.int32, (rows, 128), 1)
    st_ref[...] = jnp.where(lane == 0, mean, inv_std)
    even = jnp.where(core == 0, mine[:, 0:1], theirs[:, 0:1]) - mean
    odd = jnp.where(core == 0, theirs[:, 0:1], mine[:, 0:1]) - mean

    def grad(summed, up, vec):
        raw = inv_std * (summed + even * vec[1:2, :] + odd * vec[2:3, :])
        preact = raw + vec[0:1, :]
        gate = 1.0 / (1.0 + jnp.exp(-preact))
        pg = (up.astype(f32) * gate * (1.0 + preact * (1.0 - gate))).astype(bf16)
        wide = pg.astype(f32)
        scale = vec[1:2, :] + vec[2:3, :]
        return (
            pg,
            jnp.sum(wide * scale, axis=1, keepdims=True),
            jnp.sum(wide * raw, axis=1, keepdims=True),
        )

    pg, sum_g, sum_gu = grad(q_ref[:, :width] + got_ref[:, width : 2 * width], up_ref[...], vec_ref[...])
    pgo, sum_go, sum_guo = grad(
        q_ref[:, width : 2 * width] + got_ref[:, :width], upo_ref[...], veco_ref[...]
    )
    value = jnp.where(lane < 2, sum_g + sum_go, sum_gu + sum_guo)
    high = value.astype(bf16).astype(f32)
    tail = jnp.where(lane % 2 == 0, high, value - high).T[:PAD].astype(bf16)
    tail = jnp.concatenate([tail, jnp.zeros((PAD, feats - rows), bf16)], axis=1)
    for b in range(blocks):
        w_copies[b].wait()
        p_ref[b, :rows] = (
            lax.dot_general(pg, weight_ref[b], NT, preferred_element_type=f32)
            + lax.dot_general(pgo, other_ref[b], NT, preferred_element_type=f32)
        ).astype(bf16)
        p_ref[b, rows:] = tail


def backward(core, q, got, up, upo, vec, veco, weight, other):
    blocks, feats, _ = other.shape
    rows = q.shape[0]
    return pl.pallas_call(
        backward_kernel,
        in_specs=[SCALAR] + in_vmem(6) + [ANYWHERE] + in_vmem(1),
        out_specs=in_vmem(2),
        out_shape=[
            pltpu.VMEM((blocks, rows + PAD, feats), bf16),
            pltpu.VMEM((rows, 128), f32),
        ],
        scratch_shapes=[
            pltpu.VMEM(other.shape, bf16),
            pltpu.SemaphoreType.DMA((blocks,)),
        ],
        compiler_params=PARAMS,
        name="backward",
    )(core, q, got, up, upo, vec, veco, *far(weight), *held(other))


def finish_kernel(back_ref, x_ref, st_ref, gain_ref, target_ref, slot_ref, send_ref):
    blocks = back_ref.shape[0]
    rows, feats = x_ref.shape
    owners = send_ref.shape[0]
    total = back_ref[0].astype(f32)
    for b in range(1, blocks):
        total += back_ref[b].astype(f32)
    tail = total[rows : rows + 8, :rows]
    sums = tail.T / (2 * blocks * feats)
    first = sums[:, 0:1] + sums[:, 1:2]
    second = sums[:, 2:3] + sums[:, 3:4]
    mean, inv_std = st_ref[:, 0:1], st_ref[:, 1:2]
    unit = (x_ref[...].astype(f32) - mean) * inv_std
    grad = (inv_std * (total[:rows] * gain_ref[...] - first - unit * second)).astype(bf16)
    slots = owners * CAPACITY
    placing = lax.broadcasted_iota(jnp.int32, (slots, rows), 0) == target_ref[...]
    placed = jnp.dot(
        jnp.where(placing, 1.0, 0.0).astype(bf16), grad, preferred_element_type=f32
    ).astype(bf16)
    placed = placed.reshape(owners, CAPACITY, feats)
    for k in range(feats // 128):
        send_ref[:, k * CAPACITY : (k + 1) * CAPACITY, :] = placed[:, :, k * 128 : (k + 1) * 128]
    send_ref[:, feats // 128 * CAPACITY :, :] = jnp.broadcast_to(
        slot_ref[...][:, None, :], (owners, 2, 128)
    )


def finish(back, x, st, gain, target, slot):
    owners = slot.shape[0]
    return pl.pallas_call(
        finish_kernel,
        in_specs=in_vmem(6),
        out_specs=in_vmem(1)[0],
        out_shape=pltpu.VMEM((owners, x.shape[1] // 128 * CAPACITY + 2, 128), bf16),
        compiler_params=PARAMS,
        name="finish",
    )(*held(back, x, st, gain, target, slot))


def landing_kernel(got_ref, o_ref):
    rows, feats = o_ref.shape
    owners = got_ref.shape[0]
    slots = owners * CAPACITY
    pieces = feats // 128
    held_slots = got_ref[:, pieces * CAPACITY, :].astype(bf16)
    spread = lax.broadcasted_iota(jnp.int32, (128, slots), 0) == (
        lax.broadcasted_iota(jnp.int32, (128, slots), 1) % CAPACITY
    )
    every = jnp.dot(held_slots, jnp.where(spread, 1.0, 0.0).astype(bf16), preferred_element_type=f32)
    own = lax.broadcasted_iota(jnp.int32, (owners, slots), 0) == (
        lax.broadcasted_iota(jnp.int32, (owners, slots), 1) // CAPACITY
    )
    slot = jnp.sum(jnp.where(own, every, 0.0), axis=0, keepdims=True).astype(jnp.int32)
    landing = lax.broadcasted_iota(jnp.int32, (rows, slots), 0) == slot
    landing = jnp.where(landing, 1.0, 0.0).astype(bf16)
    for k in range(pieces):
        piece = got_ref[:, k * CAPACITY : (k + 1) * CAPACITY, :].reshape(slots, 128)
        o_ref[:, k * 128 : (k + 1) * 128] = jnp.dot(
            landing, piece, preferred_element_type=f32
        ).astype(bf16)


def land(got, rows, feats):
    return pl.pallas_call(
        landing_kernel,
        in_specs=in_vmem(1),
        out_specs=in_vmem(1)[0],
        out_shape=jax.ShapeDtypeStruct((rows, feats), bf16),
        compiler_params=PARAMS,
        name="land",
    )(*held(got))


def per_device(inputs, upstream, proj_weight, proj_bias, norm_gain, home_rows):
    rows, feats = inputs.shape
    width = upstream.shape[1]
    n_tensor, owners = lax.axis_size("tensor"), lax.axis_size("dp")
    chips = n_tensor // 2
    me = lax.axis_index("tensor")
    core = me % 2
    swap = [(t, t ^ 1) for t in range(n_tensor)]
    classes = [[2 * k + c for k in range(chips)] for c in range(2)]
    core_arr = core.reshape(1).astype(jnp.int32)

    sent = spread(inputs, chips)
    half = lax.all_to_all(sent, "tensor", 0, 0, axis_index_groups=classes, tiled=True)

    pairs = proj_weight.reshape(chips, 2, feats, width)
    gains = norm_gain.reshape(chips, 2, 1, feats)
    cut, vec = prepare(core_arr, pairs, gains, proj_bias[None])
    other = lax.ppermute(cut, "tensor", swap)
    upo = lax.ppermute(upstream, "tensor", swap)
    veco = lax.ppermute(vec, "tensor", swap)

    owner_of = home_rows // rows
    home_slot = home_rows % rows
    order_ids = jnp.arange(rows, dtype=jnp.int32)
    earlier = jnp.sum(
        ((owner_of[:, None] == owner_of[None, :]) & (order_ids[:, None] > order_ids[None, :])).astype(
            jnp.int32
        ),
        axis=1,
    )
    target = owner_of * CAPACITY + earlier
    lanes = jnp.arange(128, dtype=jnp.int32)
    held_at = (jnp.arange(owners, dtype=jnp.int32)[:, None] * CAPACITY + lanes[None, :])[:, :, None]
    match = (held_at == target[None, None, :]) & (lanes < CAPACITY)[None, :, None]
    slot = jnp.sum(jnp.where(match, home_slot[None, None, :] + 1, 0), axis=2) - 1
    slot = slot.astype(f32).astype(bf16)

    own_gain = lax.dynamic_index_in_dim(norm_gain.reshape(n_tensor, 1, feats), me, 0, False)
    half, other, upo, veco, slot, target, own_gain = lax.optimization_barrier(
        (half, other, upo, veco, slot, target, own_gain)
    )
    q = forward(core_arr, half, gains, pairs, other)
    got = lax.ppermute(q, "tensor", swap)
    parts, st = backward(core_arr, q, got, upstream, upo, vec, veco, pairs, other)
    back = lax.all_to_all(parts, "tensor", 0, 0, axis_index_groups=classes, tiled=True)
    send = finish(back, inputs, st, own_gain, target[None, :], slot)
    arrived = lax.all_to_all(send, "dp", split_axis=0, concat_axis=0, tiled=True)
    return land(arrived, rows, feats)


def solution(mesh):
    return jax.shard_map(
        per_device,
        mesh=mesh,
        in_specs=(
            P("dp", "tensor"),
            P("dp", "tensor"),
            P(None, "tensor"),
            P("tensor"),
            P(),
            P("dp"),
        ),
        out_specs=P("dp", "tensor"),
        check_vma=False,
    )
```

```python
import jax
import jax.numpy as jnp
from jax import lax
from jax.experimental import pallas as pl
from jax.experimental.pallas import tpu as pltpu
from jax.sharding import PartitionSpec as P


epsilon = 1e-05
f32, bf16 = jnp.float32, jnp.bfloat16
PAD = 8
CAPACITY = 16
NT = (((1,), (1,)), ((), ()))


def in_vmem(n):
    return [pl.BlockSpec(memory_space=pltpu.VMEM) for _ in range(n)]


def held(*arrays):
    return [pltpu.with_memory_space_constraint(a, pltpu.VMEM) for a in arrays]


def far(*arrays):
    return [pltpu.with_memory_space_constraint(a, pltpu.HBM) for a in arrays]


PARAMS = pltpu.CompilerParams(vmem_limit_bytes=16 * 1024 * 1024)


ANYWHERE = pl.BlockSpec(memory_space=pl.ANY)
SCALAR = pl.BlockSpec(memory_space=pltpu.SMEM)


def spread_kernel(x_any, o_any, x_ref, in_sem, out_sem):
    blocks, rows, _ = o_any.shape
    parts = in_sem.shape[0]
    step = rows // parts
    loads, stores = [], []
    for p in range(parts):
        span = pl.ds(p * step, step)
        loads.append(pltpu.make_async_copy(x_any.at[span], x_ref.at[span], in_sem.at[p]))
        stores.append(
            [
                pltpu.make_async_copy(x_ref.at[span], o_any.at[b, span], out_sem.at[p, b])
                for b in range(blocks)
            ]
        )
    for copy in loads:
        copy.start()
    for p in range(parts):
        loads[p].wait()
        for copy in stores[p]:
            copy.start()
    for part in stores:
        for copy in part:
            copy.wait()


def spread(x, blocks):
    return pl.pallas_call(
        spread_kernel,
        in_specs=[ANYWHERE],
        out_specs=ANYWHERE,
        out_shape=pltpu.HBM((blocks,) + x.shape, x.dtype),
        scratch_shapes=[
            pltpu.VMEM(x.shape, x.dtype),
            pltpu.SemaphoreType.DMA((4,)),
            pltpu.SemaphoreType.DMA((4, blocks)),
        ],
        compiler_params=PARAMS,
        name="spread",
    )(pltpu.with_memory_space_constraint(x, pltpu.HBM))


def prepare_kernel(core_ref, w_any, gain_ref, bias_ref, cut_any, vec_ref, w_ref, w_sem, cut_sem):
    blocks, _, feats, width = w_ref.shape
    core = core_ref[0]
    loads = [pltpu.make_async_copy(w_any.at[b], w_ref.at[b], w_sem.at[b]) for b in range(blocks)]
    stores = [
        pltpu.make_async_copy(w_ref.at[b, 1 - core], cut_any.at[b], cut_sem.at[b]) for b in range(blocks)
    ]
    for copy in loads:
        copy.start()
    row = lax.broadcasted_iota(jnp.int32, (8, feats), 0)
    totals = [jnp.zeros((8, width), f32), jnp.zeros((8, width), f32)]
    for b in range(blocks):
        loads[b].wait()
        stores[b].start()
        for c in range(2):
            gain = jnp.broadcast_to(gain_ref[b, c], (8, feats))
            high = gain.astype(bf16).astype(f32)
            middle = (gain - high).astype(bf16).astype(f32)
            low = gain - high - middle
            pieces = jnp.where(row == 0, high, jnp.where(row == 1, middle, jnp.where(row == 2, low, 0.0)))
            totals[c] += jnp.dot(pieces.astype(bf16), w_ref[b, c], preferred_element_type=f32)
    line = lax.broadcasted_iota(jnp.int32, (8, width), 0)
    even = jnp.sum(totals[0], axis=0, keepdims=True)
    odd = jnp.sum(totals[1], axis=0, keepdims=True)
    vec_ref[...] = jnp.where(line == 0, bias_ref[...], jnp.where(line == 1, even, odd))
    for copy in stores:
        copy.wait()


def prepare(core, weight, gain, bias):
    blocks, _, feats, width = weight.shape
    return pl.pallas_call(
        prepare_kernel,
        in_specs=[SCALAR, ANYWHERE] + in_vmem(2),
        out_specs=[ANYWHERE] + in_vmem(1),
        out_shape=[
            pltpu.HBM((blocks, feats, width), weight.dtype),
            jax.ShapeDtypeStruct((8, width), f32),
        ],
        scratch_shapes=[
            pltpu.VMEM(weight.shape, weight.dtype),
            pltpu.SemaphoreType.DMA((blocks,)),
            pltpu.SemaphoreType.DMA((blocks,)),
        ],
        compiler_params=PARAMS,
        name="prepare",
    )(core, *far(weight), gain, bias)


def weight_copies(core, weight_any, weight_ref, w_sem):
    blocks = weight_ref.shape[0]
    return [
        pltpu.make_async_copy(weight_any.at[b, core], weight_ref.at[b], w_sem.at[b]) for b in range(blocks)
    ]


def forward_kernel(core_ref, x_ref, gain_ref, weight_any, other_ref, q_ref, weight_ref, rows_ref, w_sem):
    blocks, rows, feats = x_ref.shape
    width = weight_ref.shape[2]
    core = core_ref[0]
    w_copies = weight_copies(core, weight_any, weight_ref, w_sem)
    for copy in w_copies:
        copy.start()
    pivot = jnp.mean(x_ref[0].astype(f32), axis=1, keepdims=True)
    total = jnp.zeros((rows, 128), f32)
    square = jnp.zeros((rows, 128), f32)
    for b in range(blocks):
        moved = x_ref[b].astype(f32) - pivot
        for j in range(0, feats, 128):
            part = moved[:, j : j + 128]
            total += part
            square += part * part
        rows_ref[:, b * feats : (b + 1) * feats] = (moved * gain_ref[b, core]).astype(bf16)
    shift = jnp.sum(total, axis=1, keepdims=True) / (blocks * feats)
    spread = jnp.sum(square, axis=1, keepdims=True) / (blocks * feats) - shift * shift
    lane = lax.broadcasted_iota(jnp.int32, (rows, 128), 1)
    q_ref[:, 2 * width :] = jnp.where(
        lane == 0, pivot, jnp.where(lane == 1, pivot + shift, jnp.maximum(spread, 0.0))
    )
    q_ref[:, width : 2 * width] = jnp.dot(
        rows_ref[...], other_ref[...].reshape(blocks * feats, width), preferred_element_type=f32
    )
    for copy in w_copies:
        copy.wait()
    q_ref[:, :width] = jnp.dot(
        rows_ref[...], weight_ref[...].reshape(blocks * feats, width), preferred_element_type=f32
    )


def forward(core, x, gain, weight, other):
    blocks, rows, feats = x.shape
    width = other.shape[2]
    x, other = held(x, other)
    return pl.pallas_call(
        forward_kernel,
        in_specs=[SCALAR] + in_vmem(2) + [ANYWHERE] + in_vmem(1),
        out_specs=in_vmem(1)[0],
        out_shape=jax.ShapeDtypeStruct((rows, 2 * width + 128), f32),
        scratch_shapes=[
            pltpu.VMEM(other.shape, bf16),
            pltpu.VMEM((rows, blocks * feats), bf16),
            pltpu.SemaphoreType.DMA((blocks,)),
        ],
        compiler_params=PARAMS,
        name="forward",
    )(core, x, gain, *far(weight), other)


def backward_kernel(
    core_ref,
    q_ref,
    got_ref,
    up_ref,
    upo_ref,
    vec_ref,
    veco_ref,
    weight_any,
    other_ref,
    p_ref,
    st_ref,
    weight_ref,
    w_sem,
):
    blocks, feats, width = weight_ref.shape
    rows = q_ref.shape[0]
    core = core_ref[0]
    w_copies = weight_copies(core, weight_any, weight_ref, w_sem)
    for copy in w_copies:
        copy.start()
    mine, theirs = q_ref[:, 2 * width :], got_ref[:, 2 * width :]
    gap = 0.5 * (mine[:, 1:2] - theirs[:, 1:2])
    mean = 0.5 * (mine[:, 1:2] + theirs[:, 1:2])
    variance = 0.5 * (mine[:, 2:3] + theirs[:, 2:3]) + gap * gap
    inv_std = lax.rsqrt(variance + epsilon)
    lane = lax.broadcasted_iota(jnp.int32, (rows, 128), 1)
    st_ref[...] = jnp.where(lane == 0, mean, inv_std)
    even = jnp.where(core == 0, mine[:, 0:1], theirs[:, 0:1]) - mean
    odd = jnp.where(core == 0, theirs[:, 0:1], mine[:, 0:1]) - mean

    def grad(summed, up, vec):
        raw = inv_std * (summed + even * vec[1:2, :] + odd * vec[2:3, :])
        preact = raw + vec[0:1, :]
        gate = 1.0 / (1.0 + jnp.exp(-preact))
        pg = (up.astype(f32) * gate * (1.0 + preact * (1.0 - gate))).astype(bf16)
        wide = pg.astype(f32)
        scale = vec[1:2, :] + vec[2:3, :]
        return (
            pg,
            jnp.sum(wide * scale, axis=1, keepdims=True),
            jnp.sum(wide * raw, axis=1, keepdims=True),
        )

    pg, sum_g, sum_gu = grad(q_ref[:, :width] + got_ref[:, width : 2 * width], up_ref[...], vec_ref[...])
    pgo, sum_go, sum_guo = grad(
        q_ref[:, width : 2 * width] + got_ref[:, :width], upo_ref[...], veco_ref[...]
    )
    value = jnp.where(lane < 2, sum_g + sum_go, sum_gu + sum_guo)
    high = value.astype(bf16).astype(f32)
    tail = jnp.where(lane % 2 == 0, high, value - high).T[:PAD].astype(bf16)
    tail = jnp.concatenate([tail, jnp.zeros((PAD, feats - rows), bf16)], axis=1)
    for b in range(blocks):
        w_copies[b].wait()
        p_ref[b, :rows] = (
            lax.dot_general(pg, weight_ref[b], NT, preferred_element_type=f32)
            + lax.dot_general(pgo, other_ref[b], NT, preferred_element_type=f32)
        ).astype(bf16)
        p_ref[b, rows:] = tail


def backward(core, q, got, up, upo, vec, veco, weight, other):
    blocks, feats, _ = other.shape
    rows = q.shape[0]
    return pl.pallas_call(
        backward_kernel,
        in_specs=[SCALAR] + in_vmem(6) + [ANYWHERE] + in_vmem(1),
        out_specs=in_vmem(2),
        out_shape=[
            pltpu.VMEM((blocks, rows + PAD, feats), bf16),
            pltpu.VMEM((rows, 128), f32),
        ],
        scratch_shapes=[
            pltpu.VMEM(other.shape, bf16),
            pltpu.SemaphoreType.DMA((blocks,)),
        ],
        compiler_params=PARAMS,
        name="backward",
    )(core, q, got, up, upo, vec, veco, *far(weight), *held(other))


def finish_kernel(back_ref, x_ref, st_ref, gain_ref, target_ref, slot_ref, send_ref):
    blocks = back_ref.shape[0]
    rows, feats = x_ref.shape
    owners = send_ref.shape[0]
    total = back_ref[0].astype(f32)
    for b in range(1, blocks):
        total += back_ref[b].astype(f32)
    tail = total[rows : rows + 8, :rows]
    sums = tail.T / (2 * blocks * feats)
    first = sums[:, 0:1] + sums[:, 1:2]
    second = sums[:, 2:3] + sums[:, 3:4]
    mean, inv_std = st_ref[:, 0:1], st_ref[:, 1:2]
    unit = (x_ref[...].astype(f32) - mean) * inv_std
    grad = (inv_std * (total[:rows] * gain_ref[...] - first - unit * second)).astype(bf16)
    slots = owners * CAPACITY
    placing = lax.broadcasted_iota(jnp.int32, (slots, rows), 0) == target_ref[...]
    placed = jnp.dot(
        jnp.where(placing, 1.0, 0.0).astype(bf16), grad, preferred_element_type=f32
    ).astype(bf16)
    placed = placed.reshape(owners, CAPACITY, feats)
    for k in range(feats // 128):
        send_ref[:, k * CAPACITY : (k + 1) * CAPACITY, :] = placed[:, :, k * 128 : (k + 1) * 128]
    send_ref[:, feats // 128 * CAPACITY :, :] = jnp.broadcast_to(
        slot_ref[...][:, None, :], (owners, 2, 128)
    )


def finish(back, x, st, gain, target, slot):
    owners = slot.shape[0]
    return pl.pallas_call(
        finish_kernel,
        in_specs=in_vmem(6),
        out_specs=in_vmem(1)[0],
        out_shape=pltpu.VMEM((owners, x.shape[1] // 128 * CAPACITY + 2, 128), bf16),
        compiler_params=PARAMS,
        name="finish",
    )(*held(back, x, st, gain, target, slot))


def landing_kernel(got_ref, o_any, o_ref, sem):
    rows, feats = o_ref.shape
    owners = got_ref.shape[0]
    slots = owners * CAPACITY
    pieces = feats // 128
    held_slots = got_ref[:, pieces * CAPACITY, :].astype(bf16)
    spread = lax.broadcasted_iota(jnp.int32, (128, slots), 0) == (
        lax.broadcasted_iota(jnp.int32, (128, slots), 1) % CAPACITY
    )
    every = jnp.dot(held_slots, jnp.where(spread, 1.0, 0.0).astype(bf16), preferred_element_type=f32)
    own = lax.broadcasted_iota(jnp.int32, (owners, slots), 0) == (
        lax.broadcasted_iota(jnp.int32, (owners, slots), 1) // CAPACITY
    )
    slot = jnp.sum(jnp.where(own, every, 0.0), axis=0, keepdims=True).astype(jnp.int32)
    landing = lax.broadcasted_iota(jnp.int32, (rows, slots), 0) == slot
    landing = jnp.where(landing, 1.0, 0.0).astype(bf16)
    copies = []
    for k in range(pieces):
        piece = got_ref[:, k * CAPACITY : (k + 1) * CAPACITY, :].reshape(slots, 128)
        span = pl.ds(k * 128, 128)
        o_ref[:, span] = jnp.dot(landing, piece, preferred_element_type=f32).astype(bf16)
        copies.append(pltpu.make_async_copy(o_ref.at[:, span], o_any.at[:, span], sem.at[k]))
        copies[k].start()
    for copy in copies:
        copy.wait()


def land(got, rows, feats):
    return pl.pallas_call(
        landing_kernel,
        in_specs=in_vmem(1),
        out_specs=ANYWHERE,
        out_shape=pltpu.HBM((rows, feats), bf16),
        scratch_shapes=[
            pltpu.VMEM((rows, feats), bf16),
            pltpu.SemaphoreType.DMA((feats // 128,)),
        ],
        compiler_params=PARAMS,
        name="land",
    )(*held(got))


def per_device(inputs, upstream, proj_weight, proj_bias, norm_gain, home_rows):
    rows, feats = inputs.shape
    width = upstream.shape[1]
    n_tensor, owners = lax.axis_size("tensor"), lax.axis_size("dp")
    chips = n_tensor // 2
    me = lax.axis_index("tensor")
    core = me % 2
    swap = [(t, t ^ 1) for t in range(n_tensor)]
    classes = [[2 * k + c for k in range(chips)] for c in range(2)]
    core_arr = core.reshape(1).astype(jnp.int32)

    sent = spread(inputs, chips)
    half = lax.all_to_all(sent, "tensor", 0, 0, axis_index_groups=classes, tiled=True)

    pairs = proj_weight.reshape(chips, 2, feats, width)
    gains = norm_gain.reshape(chips, 2, 1, feats)
    cut, vec = prepare(core_arr, pairs, gains, proj_bias[None])
    other = lax.ppermute(cut, "tensor", swap)
    upo = lax.ppermute(upstream, "tensor", swap)
    veco = lax.ppermute(vec, "tensor", swap)

    owner_of = home_rows // rows
    home_slot = home_rows % rows
    order_ids = jnp.arange(rows, dtype=jnp.int32)
    earlier = jnp.sum(
        ((owner_of[:, None] == owner_of[None, :]) & (order_ids[:, None] > order_ids[None, :])).astype(
            jnp.int32
        ),
        axis=1,
    )
    target = owner_of * CAPACITY + earlier
    lanes = jnp.arange(128, dtype=jnp.int32)
    held_at = (jnp.arange(owners, dtype=jnp.int32)[:, None] * CAPACITY + lanes[None, :])[:, :, None]
    match = (held_at == target[None, None, :]) & (lanes < CAPACITY)[None, :, None]
    slot = jnp.sum(jnp.where(match, home_slot[None, None, :] + 1, 0), axis=2) - 1
    slot = slot.astype(f32).astype(bf16)

    own_gain = lax.dynamic_index_in_dim(norm_gain.reshape(n_tensor, 1, feats), me, 0, False)
    half, other, upo, veco, slot, target, own_gain = lax.optimization_barrier(
        (half, other, upo, veco, slot, target, own_gain)
    )
    q = forward(core_arr, half, gains, pairs, other)
    got = lax.ppermute(q, "tensor", swap)
    parts, st = backward(core_arr, q, got, upstream, upo, vec, veco, pairs, other)
    back = lax.all_to_all(parts, "tensor", 0, 0, axis_index_groups=classes, tiled=True)
    send = finish(back, inputs, st, own_gain, target[None, :], slot)
    arrived = lax.all_to_all(send, "dp", split_axis=0, concat_axis=0, tiled=True)
    return land(arrived, rows, feats)


def solution(mesh):
    return jax.shard_map(
        per_device,
        mesh=mesh,
        in_specs=(
            P("dp", "tensor"),
            P("dp", "tensor"),
            P(None, "tensor"),
            P("tensor"),
            P(),
            P("dp"),
        ),
        out_specs=P("dp", "tensor"),
        check_vma=False,
    )
```

```python
import jax
import jax.numpy as jnp
from jax import lax
from jax.experimental import pallas as pl
from jax.experimental.pallas import tpu as pltpu
from jax.sharding import PartitionSpec as P


epsilon = 1e-05
f32, bf16 = jnp.float32, jnp.bfloat16
PAD = 8
CAPACITY = 16
NT = (((1,), (1,)), ((), ()))


def in_vmem(n):
    return [pl.BlockSpec(memory_space=pltpu.VMEM) for _ in range(n)]


def held(*arrays):
    return [pltpu.with_memory_space_constraint(a, pltpu.VMEM) for a in arrays]


def far(*arrays):
    return [pltpu.with_memory_space_constraint(a, pltpu.HBM) for a in arrays]


PARAMS = pltpu.CompilerParams(vmem_limit_bytes=16 * 1024 * 1024)


ANYWHERE = pl.BlockSpec(memory_space=pl.ANY)
SCALAR = pl.BlockSpec(memory_space=pltpu.SMEM)


def spread_kernel(x_any, o_any, x_ref, in_sem, out_sem):
    blocks, rows, _ = o_any.shape
    parts = in_sem.shape[0]
    step = rows // parts
    loads, stores = [], []
    for p in range(parts):
        span = pl.ds(p * step, step)
        loads.append(pltpu.make_async_copy(x_any.at[span], x_ref.at[span], in_sem.at[p]))
        stores.append(
            [
                pltpu.make_async_copy(x_ref.at[span], o_any.at[b, span], out_sem.at[p, b])
                for b in range(blocks)
            ]
        )
    for copy in loads:
        copy.start()
    for p in range(parts):
        loads[p].wait()
        for copy in stores[p]:
            copy.start()
    for part in stores:
        for copy in part:
            copy.wait()


def spread(x, blocks):
    return pl.pallas_call(
        spread_kernel,
        in_specs=[ANYWHERE],
        out_specs=ANYWHERE,
        out_shape=pltpu.HBM((blocks,) + x.shape, x.dtype),
        scratch_shapes=[
            pltpu.VMEM(x.shape, x.dtype),
            pltpu.SemaphoreType.DMA((1,)),
            pltpu.SemaphoreType.DMA((1, blocks)),
        ],
        compiler_params=PARAMS,
        name="spread",
    )(pltpu.with_memory_space_constraint(x, pltpu.HBM))


def prepare_kernel(core_ref, w_any, gain_ref, bias_ref, cut_any, vec_ref, w_ref, w_sem, cut_sem):
    blocks, _, feats, width = w_ref.shape
    core = core_ref[0]
    loads = [pltpu.make_async_copy(w_any.at[b], w_ref.at[b], w_sem.at[b]) for b in range(blocks)]
    stores = [
        pltpu.make_async_copy(w_ref.at[b, 1 - core], cut_any.at[b], cut_sem.at[b]) for b in range(blocks)
    ]
    for copy in loads:
        copy.start()
    row = lax.broadcasted_iota(jnp.int32, (8, feats), 0)
    totals = [jnp.zeros((8, width), f32), jnp.zeros((8, width), f32)]
    for b in range(blocks):
        loads[b].wait()
        stores[b].start()
        for c in range(2):
            gain = jnp.broadcast_to(gain_ref[b, c], (8, feats))
            high = gain.astype(bf16).astype(f32)
            middle = (gain - high).astype(bf16).astype(f32)
            low = gain - high - middle
            pieces = jnp.where(row == 0, high, jnp.where(row == 1, middle, jnp.where(row == 2, low, 0.0)))
            totals[c] += jnp.dot(pieces.astype(bf16), w_ref[b, c], preferred_element_type=f32)
    line = lax.broadcasted_iota(jnp.int32, (8, width), 0)
    even = jnp.sum(totals[0], axis=0, keepdims=True)
    odd = jnp.sum(totals[1], axis=0, keepdims=True)
    vec_ref[...] = jnp.where(line == 0, bias_ref[...], jnp.where(line == 1, even, odd))
    for copy in stores:
        copy.wait()


def prepare(core, weight, gain, bias):
    blocks, _, feats, width = weight.shape
    return pl.pallas_call(
        prepare_kernel,
        in_specs=[SCALAR, ANYWHERE] + in_vmem(2),
        out_specs=[ANYWHERE] + in_vmem(1),
        out_shape=[
            pltpu.HBM((blocks, feats, width), weight.dtype),
            jax.ShapeDtypeStruct((8, width), f32),
        ],
        scratch_shapes=[
            pltpu.VMEM(weight.shape, weight.dtype),
            pltpu.SemaphoreType.DMA((blocks,)),
            pltpu.SemaphoreType.DMA((blocks,)),
        ],
        compiler_params=PARAMS,
        name="prepare",
    )(core, *far(weight), gain, bias)


def weight_copies(core, weight_any, weight_ref, w_sem):
    blocks = weight_ref.shape[0]
    return [
        pltpu.make_async_copy(weight_any.at[b, core], weight_ref.at[b], w_sem.at[b]) for b in range(blocks)
    ]


def forward_kernel(core_ref, x_ref, gain_ref, weight_any, other_ref, q_ref, weight_ref, rows_ref, w_sem):
    blocks, rows, feats = x_ref.shape
    width = weight_ref.shape[2]
    core = core_ref[0]
    w_copies = weight_copies(core, weight_any, weight_ref, w_sem)
    for copy in w_copies:
        copy.start()
    pivot = jnp.mean(x_ref[0].astype(f32), axis=1, keepdims=True)
    total = jnp.zeros((rows, 128), f32)
    square = jnp.zeros((rows, 128), f32)
    for b in range(blocks):
        moved = x_ref[b].astype(f32) - pivot
        for j in range(0, feats, 128):
            part = moved[:, j : j + 128]
            total += part
            square += part * part
        rows_ref[:, b * feats : (b + 1) * feats] = (moved * gain_ref[b, core]).astype(bf16)
    shift = jnp.sum(total, axis=1, keepdims=True) / (blocks * feats)
    spread = jnp.sum(square, axis=1, keepdims=True) / (blocks * feats) - shift * shift
    lane = lax.broadcasted_iota(jnp.int32, (rows, 128), 1)
    q_ref[:, 2 * width :] = jnp.where(
        lane == 0, pivot, jnp.where(lane == 1, pivot + shift, jnp.maximum(spread, 0.0))
    )
    q_ref[:, width : 2 * width] = jnp.dot(
        rows_ref[...], other_ref[...].reshape(blocks * feats, width), preferred_element_type=f32
    )
    for copy in w_copies:
        copy.wait()
    q_ref[:, :width] = jnp.dot(
        rows_ref[...], weight_ref[...].reshape(blocks * feats, width), preferred_element_type=f32
    )


def forward(core, x, gain, weight, other):
    blocks, rows, feats = x.shape
    width = other.shape[2]
    x, other = held(x, other)
    return pl.pallas_call(
        forward_kernel,
        in_specs=[SCALAR] + in_vmem(2) + [ANYWHERE] + in_vmem(1),
        out_specs=in_vmem(1)[0],
        out_shape=jax.ShapeDtypeStruct((rows, 2 * width + 128), f32),
        scratch_shapes=[
            pltpu.VMEM(other.shape, bf16),
            pltpu.VMEM((rows, blocks * feats), bf16),
            pltpu.SemaphoreType.DMA((blocks,)),
        ],
        compiler_params=PARAMS,
        name="forward",
    )(core, x, gain, *far(weight), other)


def backward_kernel(
    core_ref,
    q_ref,
    got_ref,
    up_ref,
    upo_ref,
    vec_ref,
    veco_ref,
    weight_any,
    other_ref,
    p_ref,
    st_ref,
    weight_ref,
    w_sem,
):
    blocks, feats, width = weight_ref.shape
    rows = q_ref.shape[0]
    core = core_ref[0]
    w_copies = weight_copies(core, weight_any, weight_ref, w_sem)
    for copy in w_copies:
        copy.start()
    mine, theirs = q_ref[:, 2 * width :], got_ref[:, 2 * width :]
    gap = 0.5 * (mine[:, 1:2] - theirs[:, 1:2])
    mean = 0.5 * (mine[:, 1:2] + theirs[:, 1:2])
    variance = 0.5 * (mine[:, 2:3] + theirs[:, 2:3]) + gap * gap
    inv_std = lax.rsqrt(variance + epsilon)
    lane = lax.broadcasted_iota(jnp.int32, (rows, 128), 1)
    st_ref[...] = jnp.where(lane == 0, mean, inv_std)
    even = jnp.where(core == 0, mine[:, 0:1], theirs[:, 0:1]) - mean
    odd = jnp.where(core == 0, theirs[:, 0:1], mine[:, 0:1]) - mean

    def grad(summed, up, vec):
        raw = inv_std * (summed + even * vec[1:2, :] + odd * vec[2:3, :])
        preact = raw + vec[0:1, :]
        gate = 1.0 / (1.0 + jnp.exp(-preact))
        pg = (up.astype(f32) * gate * (1.0 + preact * (1.0 - gate))).astype(bf16)
        wide = pg.astype(f32)
        scale = vec[1:2, :] + vec[2:3, :]
        return (
            pg,
            jnp.sum(wide * scale, axis=1, keepdims=True),
            jnp.sum(wide * raw, axis=1, keepdims=True),
        )

    pg, sum_g, sum_gu = grad(q_ref[:, :width] + got_ref[:, width : 2 * width], up_ref[...], vec_ref[...])
    pgo, sum_go, sum_guo = grad(
        q_ref[:, width : 2 * width] + got_ref[:, :width], upo_ref[...], veco_ref[...]
    )
    value = jnp.where(lane < 2, sum_g + sum_go, sum_gu + sum_guo)
    high = value.astype(bf16).astype(f32)
    tail = jnp.where(lane % 2 == 0, high, value - high).T[:PAD].astype(bf16)
    tail = jnp.concatenate([tail, jnp.zeros((PAD, feats - rows), bf16)], axis=1)
    for b in range(blocks):
        w_copies[b].wait()
        p_ref[b, :rows] = (
            lax.dot_general(pg, weight_ref[b], NT, preferred_element_type=f32)
            + lax.dot_general(pgo, other_ref[b], NT, preferred_element_type=f32)
        ).astype(bf16)
        p_ref[b, rows:] = tail


def backward(core, q, got, up, upo, vec, veco, weight, other):
    blocks, feats, _ = other.shape
    rows = q.shape[0]
    return pl.pallas_call(
        backward_kernel,
        in_specs=[SCALAR] + in_vmem(6) + [ANYWHERE] + in_vmem(1),
        out_specs=in_vmem(2),
        out_shape=[
            pltpu.VMEM((blocks, rows + PAD, feats), bf16),
            pltpu.VMEM((rows, 128), f32),
        ],
        scratch_shapes=[
            pltpu.VMEM(other.shape, bf16),
            pltpu.SemaphoreType.DMA((blocks,)),
        ],
        compiler_params=PARAMS,
        name="backward",
    )(core, q, got, up, upo, vec, veco, *far(weight), *held(other))


def finish_kernel(back_ref, x_ref, st_ref, gain_ref, target_ref, slot_ref, send_ref):
    blocks = back_ref.shape[0]
    rows, feats = x_ref.shape
    owners = send_ref.shape[0]
    total = back_ref[0].astype(f32)
    for b in range(1, blocks):
        total += back_ref[b].astype(f32)
    tail = total[rows : rows + 8, :rows]
    sums = tail.T / (2 * blocks * feats)
    first = sums[:, 0:1] + sums[:, 1:2]
    second = sums[:, 2:3] + sums[:, 3:4]
    mean, inv_std = st_ref[:, 0:1], st_ref[:, 1:2]
    unit = (x_ref[...].astype(f32) - mean) * inv_std
    grad = (inv_std * (total[:rows] * gain_ref[...] - first - unit * second)).astype(bf16)
    slots = owners * CAPACITY
    placing = lax.broadcasted_iota(jnp.int32, (slots, rows), 0) == target_ref[...]
    placed = jnp.dot(
        jnp.where(placing, 1.0, 0.0).astype(bf16), grad, preferred_element_type=f32
    ).astype(bf16)
    placed = placed.reshape(owners, CAPACITY, feats)
    for k in range(feats // 128):
        send_ref[:, k * CAPACITY : (k + 1) * CAPACITY, :] = placed[:, :, k * 128 : (k + 1) * 128]
    send_ref[:, feats // 128 * CAPACITY :, :] = jnp.broadcast_to(
        slot_ref[...][:, None, :], (owners, 2, 128)
    )


def finish(back, x, st, gain, target, slot):
    owners = slot.shape[0]
    return pl.pallas_call(
        finish_kernel,
        in_specs=in_vmem(6),
        out_specs=in_vmem(1)[0],
        out_shape=pltpu.VMEM((owners, x.shape[1] // 128 * CAPACITY + 2, 128), bf16),
        compiler_params=PARAMS,
        name="finish",
    )(*held(back, x, st, gain, target, slot))


def landing_kernel(got_ref, o_ref):
    rows, feats = o_ref.shape
    owners = got_ref.shape[0]
    slots = owners * CAPACITY
    pieces = feats // 128
    held_slots = got_ref[:, pieces * CAPACITY, :].astype(bf16)
    spread = lax.broadcasted_iota(jnp.int32, (128, slots), 0) == (
        lax.broadcasted_iota(jnp.int32, (128, slots), 1) % CAPACITY
    )
    every = jnp.dot(held_slots, jnp.where(spread, 1.0, 0.0).astype(bf16), preferred_element_type=f32)
    own = lax.broadcasted_iota(jnp.int32, (owners, slots), 0) == (
        lax.broadcasted_iota(jnp.int32, (owners, slots), 1) // CAPACITY
    )
    slot = jnp.sum(jnp.where(own, every, 0.0), axis=0, keepdims=True).astype(jnp.int32)
    landing = lax.broadcasted_iota(jnp.int32, (rows, slots), 0) == slot
    landing = jnp.where(landing, 1.0, 0.0).astype(bf16)
    for k in range(pieces):
        piece = got_ref[:, k * CAPACITY : (k + 1) * CAPACITY, :].reshape(slots, 128)
        o_ref[:, k * 128 : (k + 1) * 128] = jnp.dot(
            landing, piece, preferred_element_type=f32
        ).astype(bf16)


def land(got, rows, feats):
    return pl.pallas_call(
        landing_kernel,
        in_specs=in_vmem(1),
        out_specs=in_vmem(1)[0],
        out_shape=jax.ShapeDtypeStruct((rows, feats), bf16),
        compiler_params=PARAMS,
        name="land",
    )(*held(got))


def per_device(inputs, upstream, proj_weight, proj_bias, norm_gain, home_rows):
    rows, feats = inputs.shape
    width = upstream.shape[1]
    n_tensor, owners = lax.axis_size("tensor"), lax.axis_size("dp")
    chips = n_tensor // 2
    me = lax.axis_index("tensor")
    core = me % 2
    swap = [(t, t ^ 1) for t in range(n_tensor)]
    classes = [[2 * k + c for k in range(chips)] for c in range(2)]
    core_arr = core.reshape(1).astype(jnp.int32)

    sent = spread(inputs, chips)
    half = lax.all_to_all(sent, "tensor", 0, 0, axis_index_groups=classes, tiled=True)

    pairs = proj_weight.reshape(chips, 2, feats, width)
    gains = norm_gain.reshape(chips, 2, 1, feats)
    cut, vec = prepare(core_arr, pairs, gains, proj_bias[None])
    other = lax.ppermute(cut, "tensor", swap)
    upo = lax.ppermute(upstream, "tensor", swap)
    veco = lax.ppermute(vec, "tensor", swap)

    owner_of = home_rows // rows
    home_slot = home_rows % rows
    order_ids = jnp.arange(rows, dtype=jnp.int32)
    earlier = jnp.sum(
        ((owner_of[:, None] == owner_of[None, :]) & (order_ids[:, None] > order_ids[None, :])).astype(
            jnp.int32
        ),
        axis=1,
    )
    target = owner_of * CAPACITY + earlier
    lanes = jnp.arange(128, dtype=jnp.int32)
    held_at = (jnp.arange(owners, dtype=jnp.int32)[:, None] * CAPACITY + lanes[None, :])[:, :, None]
    match = (held_at == target[None, None, :]) & (lanes < CAPACITY)[None, :, None]
    slot = jnp.sum(jnp.where(match, home_slot[None, None, :] + 1, 0), axis=2) - 1
    slot = slot.astype(f32).astype(bf16)

    own_gain = lax.dynamic_index_in_dim(norm_gain.reshape(n_tensor, 1, feats), me, 0, False)
    half, other, upo, veco, slot, target, own_gain = lax.optimization_barrier(
        (half, other, upo, veco, slot, target, own_gain)
    )
    q = forward(core_arr, half, gains, pairs, other)
    got = lax.ppermute(q, "tensor", swap)
    parts, st = backward(core_arr, q, got, upstream, upo, vec, veco, pairs, other)
    back = lax.all_to_all(parts, "tensor", 0, 0, axis_index_groups=classes, tiled=True)
    send = finish(back, inputs, st, own_gain, target[None, :], slot)
    arrived = lax.all_to_all(send, "dp", split_axis=0, concat_axis=0, tiled=True)
    return land(arrived, rows, feats)


def solution(mesh):
    return jax.shard_map(
        per_device,
        mesh=mesh,
        in_specs=(
            P("dp", "tensor"),
            P("dp", "tensor"),
            P(None, "tensor"),
            P("tensor"),
            P(),
            P("dp"),
        ),
        out_specs=P("dp", "tensor"),
        check_vma=False,
    )
```
